32 devices in a mesh: rep: 2 (over x), atom: 16 (over z, y, core).
Axes of the slice: x: 2, y: 2, z: 4, core: 2. Of those that a mesh axis runs over, the one named last changes fastest.
Arguments:
- features: bfloat16 [4096, 256], P(('rep', 'atom')), parts along dimension 0, may hold values from -6 to 6
- fractional: float32 [3, 4096], P(None, ('rep', 'atom')), parts along dimension 1, may hold values from 0 to 1, as said below
- distances: float32 [64, 4096], P(None, ('rep', 'atom')), parts along dimension 1, may hold values from 0.8 to 4.8
- neighbours: int32 [64, 4096], P(None, ('rep', 'atom')), parts along dimension 1, may hold values from 0 to 383
- edge_mask: int32 [64, 4096], P(None, ('rep', 'atom')), parts along dimension 1, may hold values 0 or 1
- wave_index: int32 [3, 2048], replicated, may hold values from -6 to 6
- w_rbf: bfloat16 [2, 64, 512], replicated, may hold values from -1.5 to 1.5
- w_filter: bfloat16 [2, 512, 256], replicated, may hold values from -0.25 to 0.25
- w_mixing: bfloat16 [2, 256, 256], replicated, may hold values from -0.375 to 0.375
- w_short: bfloat16 [2, 256, 256], replicated, may hold values from -0.375 to 0.375
- w_long: bfloat16 [2, 256, 256], replicated, may hold values from -0.375 to 0.375
Outputs:
- features_out: bfloat16 [4096, 256], P(('rep', 'atom')), parts along dimension 0
The draws below stay inside these ranges and needn't reach their ends.
There are 2 independent parts, one for each index of `rep`. The reference program is written for one: setup_inputs(seed, part) draws one part's arguments, and reference() takes and returns one part's arrays. A program takes and returns all parts, laid end to end along the dimension named above; an argument that names none is the same for every part. Nothing has to cross between parts.
Inputs may be any that keep to these rules, and one draw needn't show every extreme that they name: neighbours[n, i] indexes the concatenation of the previous brick, atom i's own brick and the next brick, cyclic over the 16 bricks. `fractional`: atom i has its z coordinate within brick i // 128, that is between (i // 128) * 128 / 2048 and one brick further.
All inputs are finite; a program needn't handle non-finite values. No bound on the sum of `edge_mask` on one device may be relied on, other than what follows from the above.
Results may differ from the reference program's by a relative error of at most 0.01.
Values may be sent and summed in bfloat16 or wider, within the bound.
No kernel may reach another device: no remote copies, remote signals or barrier semaphores. Data moves between devices by JAX's collectives and lax.ppermute only.
A program may use at most 64 MiB of HBM per device.

```python
import math
import jax
import jax.numpy as jnp
from jax import lax

F = 256
H = 512
R = 64
K = 2048
NB = 64
LAYERS = 2
ATOM_DEV = 128
ATOMS = 2048


def draw_fractional(key, part):
    base = jax.random.fold_in(key, 7)
    first, second = jax.random.split(base)
    plane = jax.random.uniform(first, (2, ATOMS), jnp.float32)
    offset = jax.random.uniform(second, (ATOMS,), jnp.float32)
    brick = (jnp.arange(ATOMS) // ATOM_DEV).astype(jnp.float32)
    height = (brick + offset) * (ATOM_DEV / ATOMS)
    return jnp.concatenate([plane, height[None, :]], axis=0)


def with_ends(result, stream_key, least, high):
    dims = result.shape
    spot = [jax.random.randint(jax.random.fold_in(stream_key, axis), (), 0, dims[axis]) for axis in range(len(dims))]
    result = result.at[tuple(spot)].set(least)
    longest = dims.index(max(dims))
    spot[longest] = (spot[longest] + 1) % dims[longest]
    return result.at[tuple(spot)].set(high)


def block_scale(key, extent, cuts, low, largest):
    gain = 1.0
    for axis_at, parts in cuts:
        heights = jax.random.uniform(jax.random.fold_in(jax.random.fold_in(key, 6), axis_at), (parts,), jnp.float32, low / len(cuts), largest / len(cuts))
        gain = gain * jnp.repeat(jnp.exp(heights), extent[axis_at] // parts).reshape((-1,) + (1,) * (len(extent) - 1 - axis_at))
    return gain


def scatter_about(key, extent, scale, limit, cuts=(), held_as=jnp.bfloat16):
    drawn = jax.random.normal(key, extent, jnp.float32) * scale
    if len(cuts) > 0:
        drawn = block_scale(key, extent, cuts, -0.22, 0.18) * drawn
    return jnp.clip(drawn, min=-limit, max=limit).astype(held_as)


def setup_inputs(seed: int = 0, part: int = 0) -> dict:
    seeds = jax.random.split(jax.random.key(seed), 12)
    own_keys = jax.random.split(jax.random.fold_in(seeds[11], part), 12)
    return {
        "features": scatter_about(own_keys[0], (ATOMS, F), 1.0, 6.0, ((0, 16),)),
        "fractional": draw_fractional(jax.random.fold_in(jax.random.fold_in(seeds[11], part), 71), part),
        "distances": jnp.clip(0.8 + 4 * jax.random.uniform(own_keys[2], (NB, ATOMS), jnp.float32) ** block_scale(own_keys[2], (NB, ATOMS), ((1, 16),), -0.2, 0.2), 0.8, 4.8),
        "neighbours": with_ends(jax.random.randint(own_keys[3], (NB, ATOMS), 0, 3 * ATOM_DEV), jax.random.fold_in(own_keys[3], 1), 0, (3 * ATOM_DEV) - 1).astype(jnp.int32),
        "edge_mask": with_ends((jax.random.randint(own_keys[4], (NB, ATOMS), 0, 4) < 3).astype(jnp.int32), jax.random.fold_in(own_keys[4], 1), 0, 1),
        "wave_index": with_ends(jax.random.randint(seeds[5], (3, K), -6, 7), jax.random.fold_in(seeds[5], 1), -6, 6).astype(jnp.int32),
        "w_rbf": scatter_about(seeds[6], (LAYERS, R, H), (R // 4) ** -0.5, 1.5),
        "w_filter": scatter_about(seeds[7], (LAYERS, H, F), H ** -0.5, 0.25),
        "w_mixing": scatter_about(seeds[8], (LAYERS, F, F), F ** -0.5, 0.375),
        "w_short": scatter_about(seeds[9], (LAYERS, F, F), F ** -0.5, 0.375),
        "w_long": scatter_about(seeds[10], (LAYERS, F, F), F ** -0.5, 0.375),
    }


slot_group = 8
tau_value = 2.0 * math.pi

def edge_basis(distance, count):
    centers = 0.5 + 4.5 * jnp.arange(count, dtype=jnp.float32) / (count - 1)
    offset = distance[..., None] - centers
    return jnp.exp(-4.0 * offset * offset).astype(jnp.bfloat16)

def envelope(distance):
    return 0.5 * (jnp.cos(math.pi * distance / 5.0) + 1.0)

def messages(table, index, distance, edge_weight, rbf_weight, filter_weight):
    groups = index.shape[0] // slot_group
    rows = index.shape[1]
    count = rbf_weight.shape[0]

    def advance(total, pieces):
        index_part, distance_part, weight_part = pieces
        basis = edge_basis(distance_part, count).reshape(slot_group * rows, count)
        inner = jax.nn.silu(jnp.dot(basis, rbf_weight, preferred_element_type=jnp.float32)).astype(jnp.bfloat16)
        filters = jnp.dot(inner, filter_weight, preferred_element_type=jnp.float32).reshape(slot_group, rows, -1)
        filters = filters * weight_part[:, :, None]
        gathered = jnp.take(table, index_part, axis=0).astype(jnp.float32)
        return (total + lax.optimization_barrier(jnp.sum(filters * gathered, axis=0)), None)
    start = jnp.zeros((rows, filter_weight.shape[1]), jnp.float32)
    total, _ = lax.scan(advance, start, (index.reshape(groups, slot_group, rows), distance.reshape(groups, slot_group, rows), edge_weight.reshape(groups, slot_group, rows)))
    return total

def transposed(left, right):
    return lax.dot_general(left, right, (((0,), (0,)), ((), ())), preferred_element_type=jnp.float32)

def reference(features, fractional, distances, neighbours, edge_mask, wave_index, w_rbf, w_filter, w_mixing, w_short, w_long):
    atoms_all = features.shape[0]
    width = features.shape[1]
    brick_start = (jnp.arange(atoms_all, dtype=jnp.int32) // ATOM_DEV * ATOM_DEV).astype(jnp.int32)
    partner = ((brick_start[None, :] - ATOM_DEV + neighbours) % atoms_all).astype(jnp.int32)
    edge_weight = envelope(distances) * edge_mask.astype(jnp.float32)
    wave_float = wave_index.astype(jnp.float32)
    angle = tau_value * (fractional[0][:, None] * wave_float[0][None, :] + fractional[1][:, None] * wave_float[1][None, :] + fractional[2][:, None] * wave_float[2][None, :])
    cosine = jnp.cos(angle).astype(jnp.bfloat16)
    sine = jnp.sin(angle).astype(jnp.bfloat16)
    gains = 1.0 / (1.0 + (wave_float[0] * wave_float[0] + wave_float[1] * wave_float[1] + wave_float[2] * wave_float[2]) / 16.0)
    state = features
    for layer_index in range(LAYERS):
        message = messages(state, partner, distances, edge_weight, w_rbf[layer_index], w_filter[layer_index]).astype(jnp.bfloat16)
        structure = jnp.concatenate([transposed(cosine, state), transposed(sine, state)], axis=1)
        scaled = (structure * gains[:, None] / jnp.sqrt(jnp.float32(atoms_all))).astype(jnp.bfloat16)
        waves = scaled.shape[0]
        potential = jnp.dot(scaled.reshape(2 * waves, width), w_mixing[layer_index], preferred_element_type=jnp.float32)
        potential = potential.reshape(waves, 2 * width).astype(jnp.bfloat16)
        field = jnp.dot(cosine, potential[:, :width], preferred_element_type=jnp.float32)
        field = field + jnp.dot(sine, potential[:, width:], preferred_element_type=jnp.float32)
        field = (field * (4.0 / math.sqrt(K))).astype(jnp.bfloat16)
        update = jnp.dot(message, w_short[layer_index], preferred_element_type=jnp.float32)
        update = update + jnp.dot(field, w_long[layer_index], preferred_element_type=jnp.float32)
        state = (state.astype(jnp.float32) + jax.nn.silu(update)).astype(jnp.bfloat16)
    return state
```

```python
import functools
import math

import jax
import jax.numpy as jnp
from jax import lax
from jax.experimental import pallas as pl
from jax.experimental.pallas import tpu as pltpu
from jax.sharding import PartitionSpec as P


slot_group = 8
reach = 6
orders = reach + 1
columns = 16
plane = (reach + 2) * columns
extra_rows = 16
BF = jnp.bfloat16
F32 = jnp.float32


def dot(a, b):
    return jnp.dot(a, b, preferred_element_type=F32)


def dot_dims(a, b, ca, cb):
    return lax.dot_general(a, b, (((ca,), (cb,)), ((), ())), preferred_element_type=F32)


def turn_trig(turns):
    part = turns - jnp.round(turns)
    angle = part * (2.0 * math.pi)
    square = angle * angle
    cosine = jnp.full_like(square, 1.0 / math.factorial(20))
    for n in range(18, -2, -2):
        cosine = cosine * -square + 1.0 / math.factorial(n)
    sine = jnp.full_like(square, 1.0 / math.factorial(21))
    for n in range(19, -1, -2):
        sine = sine * -square + 1.0 / math.factorial(n)
    return cosine, sine * angle


def plane_phases(position):
    rows = position.shape[1]
    x, y = position[0:1], position[1:2]
    first = lax.broadcasted_iota(jnp.int32, (8, rows), 0).astype(F32)
    second = lax.broadcasted_iota(jnp.int32, (columns, rows), 0).astype(F32) - reach
    xc, xs = turn_trig(first * x)
    yc, ys = turn_trig(second * y)
    cosines, sines = [], []
    for a in range(plane // columns):
        pc, ps = xc[a : a + 1], xs[a : a + 1]
        cosines.append(pc * yc - ps * ys)
        sines.append(pc * ys + ps * yc)
    return jnp.concatenate(cosines, axis=0), jnp.concatenate(sines, axis=0)


def prepare_kernel(wave_ref, position_ref, left_ref, zc_ref, zs_ref):
    waves = wave_ref.shape[1]
    m0, m1, m2 = wave_ref[0:1, :], wave_ref[1:2, :], wave_ref[2:3, :]
    flip = jnp.logical_or(m0 < 0, jnp.logical_and(m0 == 0, m1 < 0))
    sign = jnp.where(flip, -1, 1)
    code = m0 * sign * columns + m1 * sign + reach
    height = m2 * sign
    row = lax.broadcasted_iota(jnp.int32, (plane, waves), 0)
    chosen = jnp.where(row == code, 1.0, 0.0).astype(BF)
    order = lax.broadcasted_iota(jnp.int32, (16, waves), 0)
    weight = jnp.where(order < 8, 1, jnp.where(height < 0, -1, 1)).astype(F32)
    picked = jnp.where(jnp.abs(height) == order % 8, weight, 0.0).astype(BF)
    count = dot_dims(picked, chosen, 1, 1)
    lane = lax.broadcasted_iota(jnp.int32, (16, plane), 1)
    k0 = (lane // columns).astype(F32)
    k1 = (lane % columns - reach).astype(F32)
    k2 = (lax.broadcasted_iota(jnp.int32, (16, plane), 0) % 8).astype(F32)
    strength = count / (1.0 + (k0 * k0 + k1 * k1 + k2 * k2) / 16.0)

    rows = position_ref.shape[1]
    position = position_ref[...]
    cosine, sine = plane_phases(position)
    cosine, sine = cosine.T, sine.T
    for m in range(orders):
        even = strength[m : m + 1]
        left_ref[m, :, :plane] = (cosine * even).astype(BF)
        left_ref[m, :, plane:] = (sine * even).astype(BF)
        if m:
            odd = strength[8 + m : 9 + m]
            left_ref[reach + m, :, :plane] = (sine * -odd).astype(BF)
            left_ref[reach + m, :, plane:] = (cosine * odd).astype(BF)
    zc, zs = turn_trig(position[2:3])
    zc_ref[...] = jnp.broadcast_to(zc, (rows, rows)).T
    zs_ref[...] = jnp.broadcast_to(zs, (rows, rows)).T


def prepare(wave_index, position):
    rows = position.shape[1]
    return pl.pallas_call(
        prepare_kernel,
        out_shape=(
            jax.ShapeDtypeStruct((2 * reach + 1, rows, 2 * plane), BF),
            jax.ShapeDtypeStruct((rows, rows), F32),
            jax.ShapeDtypeStruct((rows, rows), F32),
        ),
        name="prepare",
    )(wave_index, position)


def coupling_kernel(places, rows, left_ref, zc_ref, zs_ref, *refs):
    count = max(p[0] for p in places) + 1
    packed, out_ref, right_ref, part_ref = refs[:count], refs[count], refs[count + 1], refs[count + 2]
    tile = 32
    for pair in range(0, len(places), 2):
        span = min(2, len(places) - pair)
        heights = []
        for side in range(span):
            which, start = places[pair + side]
            block = packed[which][start + rows : start + rows + extra_rows, :].astype(F32)
            position = (block[0:3, :rows] + block[0:3, rows : 2 * rows]) + block[3:6, :rows]
            cosine, sine = plane_phases(position)
            at = slice(side * rows, (side + 1) * rows)
            right_ref[:plane, at] = cosine.astype(BF)
            right_ref[plane:, at] = sine.astype(BF)
            heights.append(turn_trig(position[2:3]))
        wide = span * rows
        for m in range(2 * reach + 1):
            part_ref[m, :, :wide] = dot(left_ref[m], right_ref[:, :wide])
        for side in range(span):
            zc, zs = heights[side]
            at = slice(side * rows, (side + 1) * rows)
            for top in range(0, rows, tile):
                own = slice(top, top + tile)
                oc, os = zc_ref[own, :], zs_ref[own, :]
                c1 = oc * zc + os * zs
                s1 = os * zc - oc * zs
                twice = c1 + c1
                total = part_ref[0, own, at] + c1 * part_ref[1, own, at] + s1 * part_ref[reach + 1, own, at]
                c0, s0 = jnp.ones_like(c1), jnp.zeros_like(s1)
                for m in range(2, orders):
                    c0, c1 = c1, twice * c1 - c0
                    s0, s1 = s1, twice * s1 - s0
                    total = total + c1 * part_ref[m, own, at] + s1 * part_ref[reach + m, own, at]
                out_ref[own, pair * rows + side * rows : pair * rows + (side + 1) * rows] = total.astype(BF)


def coupling(prepared, arrays, places, rows):
    left, zc, zs = prepared
    return pl.pallas_call(
        functools.partial(coupling_kernel, tuple(places), rows),
        out_shape=jax.ShapeDtypeStruct((rows, len(places) * rows), BF),
        scratch_shapes=[
            pltpu.VMEM((2 * plane, 2 * rows), BF),
            pltpu.VMEM((2 * reach + 1, rows, 2 * rows), F32),
        ],
        name="coupling",
    )(left, zc, zs, *arrays)


def filter_kernel(distance_ref, rbf_ref, filter_ref, out_ref):
    group, rows = distance_ref.shape
    count = rbf_ref.shape[0]
    step = lax.broadcasted_iota(jnp.int32, (count, rows), 0).astype(F32)
    centers = 0.5 + 4.5 * step / (count - 1)
    pieces = []
    for s in range(group):
        offset = distance_ref[s : s + 1, :] - centers
        pieces.append(jnp.exp(-4.0 * offset * offset).astype(BF))
    basis = jnp.concatenate(pieces, axis=1)
    half = dot_dims(basis, rbf_ref[...] * jnp.asarray(0.5, BF), 0, 0)
    inner = (half + half * jnp.tanh(half)).astype(BF)
    out_ref[...] = dot(inner, filter_ref[...]).astype(BF).reshape(out_ref.shape)


def filters_of(distances, w_rbf, w_filter, layer):
    slots, rows = distances.shape
    width = w_filter.shape[2]
    return pl.pallas_call(
        filter_kernel,
        out_shape=jax.ShapeDtypeStruct((slots, rows, width), BF),
        grid=(slots // slot_group,),
        in_specs=[
            pl.BlockSpec((slot_group, rows), lambda g: (g, 0)),
            pl.BlockSpec((None,) + w_rbf.shape[1:], lambda g: (layer, 0, 0)),
            pl.BlockSpec((None,) + w_filter.shape[1:], lambda g: (layer, 0, 0)),
        ],
        out_specs=pl.BlockSpec((slot_group, rows, width), lambda g: (g, 0, 0)),
        name="filters",
    )(distances, w_rbf, w_filter)


def message_kernel(index_ref, weight_ref, table_ref, filter_ref, out_ref, total_ref):
    _, rows, group = index_ref.shape
    reachable, width = table_ref.shape
    lane = lax.broadcasted_iota(jnp.int32, (rows, reachable), 1)
    picks = []
    for s in range(group):
        picks.append(
            jnp.where(lane == index_ref[0, :, s : s + 1], weight_ref[0, :, s : s + 1], 0.0).astype(BF)
        )
    gathered = dot(jnp.concatenate(picks, axis=0), table_ref[...]).reshape(group, rows, width)
    part = jnp.sum(gathered * filter_ref[...].astype(F32), axis=0)

    @pl.when(pl.program_id(0) == 0)
    def _():
        total_ref[...] = part

    @pl.when(pl.program_id(0) > 0)
    def _():
        total_ref[...] += part

    @pl.when(pl.program_id(0) == pl.num_programs(0) - 1)
    def _():
        out_ref[...] = total_ref[...].astype(BF)


def messages(index, weight, table, filters):
    groups, rows, group = index.shape
    width = table.shape[1]
    return pl.pallas_call(
        message_kernel,
        out_shape=jax.ShapeDtypeStruct((rows, width), BF),
        grid=(groups,),
        in_specs=[
            pl.BlockSpec((1, rows, group), lambda g: (g, 0, 0)),
            pl.BlockSpec((1, rows, group), lambda g: (g, 0, 0)),
            pl.BlockSpec(table.shape, lambda g: (0, 0)),
            pl.BlockSpec((group, rows, width), lambda g: (g, 0, 0)),
        ],
        out_specs=pl.BlockSpec((rows, width), lambda g: (0, 0)),
        scratch_shapes=[pltpu.VMEM((rows, width), F32)],
        name="messages",
    )(index, weight, table, filters)


def update_kernel(places, before, after, own_ref, message_ref, mixing_ref, short_ref, long_ref, *refs):
    rows, width = own_ref.shape
    counts = sorted({p[0] for p in places})
    pairs = len({p[2] for p in places})
    matrices, states, out_ref = refs[:pairs], refs[pairs : pairs + len(counts)], refs[-1]
    total = jnp.zeros((rows, width), F32)
    for which, start, matrix, column in places:
        total = total + dot(
            matrices[matrix][:, column * rows : (column + 1) * rows], states[which][start : start + rows, :]
        )
    potential = dot((total * before).astype(BF), mixing_ref[...]).astype(BF)
    field = (potential.astype(F32) * after).astype(BF)
    half = 0.5 * (dot(message_ref[...], short_ref[...]) + dot(field, long_ref[...]))
    out_ref[...] = (own_ref[...].astype(F32) + (half + half * jnp.tanh(half))).astype(BF)


def update(own, message, weights, layer, matrices, arrays, places, before, after):
    rows, width = own.shape
    square = pl.BlockSpec((None, width, width), lambda i: (layer, 0, 0))
    whole = lambda x: pl.BlockSpec(x.shape, lambda i: (0,) * x.ndim)
    return pl.pallas_call(
        functools.partial(update_kernel, tuple(places), before, after),
        out_shape=jax.ShapeDtypeStruct((rows, width), BF),
        grid=(1,),
        in_specs=[whole(own), whole(message), square, square, square]
        + [whole(m) for m in matrices]
        + [whole(a) for a in arrays],
        out_specs=pl.BlockSpec((rows, width), lambda i: (0, 0)),
        name="update",
    )(own, message, *weights, *matrices, *arrays)


def swap(x, mask):
    count = lax.axis_size("atom")
    return lax.ppermute(x, "atom", [(i, i ^ mask) for i in range(count)])


def schedule(count):
    stages = []
    have = [0]
    bits = [1 << n for n in range(count.bit_length() - 1)][::-1]
    if len(bits) >= 4:
        far, near, side = bits[0], bits[1], bits[2]
        stages.append([(far + near, [0]), (far, [0]), (near, [0]), (side, [0])])
        stages.append([(side, [far + near, far, near]), ] )
        have = [0, far + near, far, near, side, side + far + near, side + far, side + near]
        bits = bits[3:]
    for bit in bits:
        stages.append([(bit, list(have))])
        have = have + [q ^ bit for q in have]
    return stages


def gather_all(block, stages):
    size = block.shape[0]
    arrays, places = [block], {0: (0, 0)}
    for stage in stages:
        fresh = {}
        for mask, wanted in stage:
            parts = [
                lax.slice_in_dim(arrays[places[q][0]], places[q][1], places[q][1] + size, axis=0)
                for q in wanted
            ]
            sent = parts[0] if len(parts) == 1 else jnp.concatenate(parts, axis=0)
            arrays.append(swap(sent, mask))
            for n, q in enumerate(wanted):
                fresh[q ^ mask] = (len(arrays) - 1, n * size)
        places.update(fresh)
    return arrays, places


def neighbour_table(own, even):
    count = lax.axis_size("atom")
    close = swap(own, 1)
    far = lax.ppermute(
        own, "atom", [(i, (i + (count - 1 if i % 2 == 0 else 1)) % count) for i in range(count)]
    )
    return jnp.concatenate([jnp.where(even, far, close), own, jnp.where(even, close, far)], axis=0)


def thirds(position):
    top = lax.reduce_precision(position, 8, 7)
    rest = position - top
    middle = lax.reduce_precision(rest, 8, 7)
    return top, middle, rest - middle


def per_device(
    features,
    fractional,
    distances,
    neighbours,
    edge_mask,
    wave_index,
    w_rbf,
    w_filter,
    w_mixing,
    w_short,
    w_long,
):
    rows, width = features.shape
    slots = neighbours.shape[0]
    bricks = lax.axis_size("atom")
    before = 1.0 / math.sqrt(rows * bricks)
    after = 4.0 / math.sqrt(wave_index.shape[1])
    even = lax.axis_index("atom") % 2 == 0
    stages = schedule(bricks)

    top, middle, low = thirds(fractional)
    tail = jnp.concatenate(
        [
            jnp.concatenate([top, middle], axis=1),
            jnp.concatenate([low, jnp.zeros_like(low)], axis=1),
            jnp.zeros((extra_rows - 6, 2 * rows), F32),
        ],
        axis=0,
    ).astype(BF)
    packed = jnp.concatenate([features, tail], axis=0)

    weight = 0.5 * (jnp.cos(math.pi * distances / 5.0) + 1.0) * edge_mask.astype(F32)
    shape = (slots // slot_group, slot_group, rows)
    weight = jnp.swapaxes(weight.reshape(shape), 1, 2)
    index = jnp.swapaxes(neighbours.reshape(shape), 1, 2)

    prepared = prepare(wave_index, fractional)
    state = features
    matrices = None
    for layer in range(w_rbf.shape[0]):
        filters = filters_of(distances, w_rbf, w_filter, layer)
        arrays, places = gather_all(packed if layer == 0 else state, stages)
        table = neighbour_table(state, even)
        message = messages(index, weight, table, filters)
        kept = sorted(places)
        early = [q for q in kept if places[q][0] < len(arrays) - 1]
        late = [q for q in kept if places[q][0] == len(arrays) - 1]
        if layer == 0:
            matrices = [
                coupling(prepared, arrays[:-1], [places[q] for q in early], rows),
                coupling(prepared, arrays[-1:], [(0, places[q][1]) for q in late], rows),
            ]
        spots = [places[q] + (0, n) for n, q in enumerate(early)] + [
            places[q] + (1, n) for n, q in enumerate(late)
        ]
        state = update(
            state, message, (w_mixing, w_short, w_long), layer, matrices, arrays, spots, before, after
        )
    return state


def solution(mesh):
    along = P(None, ("rep", "atom"))
    in_specs = (P(("rep", "atom"), None), along, along, along, along) + (P(),) * 6
    return jax.shard_map(
        per_device, mesh=mesh, in_specs=in_specs, out_specs=P(("rep", "atom"), None), check_vma=False
    )
```

```python
import functools
import math

import jax
import jax.numpy as jnp
from jax import lax
from jax.experimental import pallas as pl
from jax.experimental.pallas import tpu as pltpu
from jax.sharding import PartitionSpec as P


filter_group = 32
message_group = 16
reach = 6
orders = reach + 1
columns = 16
plane = (reach + 2) * columns
extra_rows = 16
limit = pltpu.CompilerParams(vmem_limit_bytes=20 << 20)
BF = jnp.bfloat16
F32 = jnp.float32


def dot(a, b):
    return jnp.dot(a, b, preferred_element_type=F32)


def dot_dims(a, b, ca, cb):
    return lax.dot_general(a, b, (((ca,), (cb,)), ((), ())), preferred_element_type=F32)


def turn_trig(turns):
    part = turns - jnp.round(turns)
    angle = part * (2.0 * math.pi)
    square = angle * angle
    cosine = jnp.full_like(square, 1.0 / math.factorial(20))
    for n in range(18, -2, -2):
        cosine = cosine * -square + 1.0 / math.factorial(n)
    sine = jnp.full_like(square, 1.0 / math.factorial(21))
    for n in range(19, -1, -2):
        sine = sine * -square + 1.0 / math.factorial(n)
    return cosine, sine * angle


def plane_phases(position):
    rows = position.shape[1]
    x, y = position[0:1], position[1:2]
    first = lax.broadcasted_iota(jnp.int32, (8, rows), 0).astype(F32)
    second = lax.broadcasted_iota(jnp.int32, (columns, rows), 0).astype(F32) - reach
    xc, xs = turn_trig(first * x)
    yc, ys = turn_trig(second * y)
    cosines, sines = [], []
    for a in range(plane // columns):
        pc, ps = xc[a : a + 1], xs[a : a + 1]
        cosines.append(pc * yc - ps * ys)
        sines.append(pc * ys + ps * yc)
    return jnp.concatenate(cosines, axis=0), jnp.concatenate(sines, axis=0)


def in_hbm(x):
    return pltpu.with_memory_space_constraint(x, pltpu.HBM)


def whole(x):
    return pl.BlockSpec(x.shape, lambda i: (0,) * len(x.shape))


def prepare_kernel(wave_ref, position_ref, own_ref, packed_ref, left_ref, zc_ref, zs_ref):
    rows = position_ref.shape[1]
    position = position_ref[...]
    top = position.astype(BF)
    rest = position - top.astype(F32)
    middle = rest.astype(BF)
    low = (rest - middle.astype(F32)).astype(BF)
    blank = jnp.zeros((extra_rows, 2 * rows), BF)
    packed_ref[:rows, :] = own_ref[...]
    packed_ref[rows:, :] = blank
    packed_ref[rows : rows + 3, :rows] = top
    packed_ref[rows : rows + 3, rows : 2 * rows] = middle
    packed_ref[rows + 3 : rows + 6, :rows] = low

    waves = wave_ref.shape[1]
    m0, m1, m2 = wave_ref[0:1, :], wave_ref[1:2, :], wave_ref[2:3, :]
    flip = jnp.logical_or(m0 < 0, jnp.logical_and(m0 == 0, m1 < 0))
    sign = jnp.where(flip, -1, 1)
    code = m0 * sign * columns + m1 * sign + reach
    height = m2 * sign
    row = lax.broadcasted_iota(jnp.int32, (plane, waves), 0)
    chosen = jnp.where(row == code, 1.0, 0.0).astype(BF)
    order = lax.broadcasted_iota(jnp.int32, (16, waves), 0)
    weight = jnp.where(order < 8, 1, jnp.where(height < 0, -1, 1)).astype(F32)
    picked = jnp.where(jnp.abs(height) == order % 8, weight, 0.0).astype(BF)
    count = dot_dims(picked, chosen, 1, 1)
    lane = lax.broadcasted_iota(jnp.int32, (16, plane), 1)
    k0 = (lane // columns).astype(F32)
    k1 = (lane % columns - reach).astype(F32)
    k2 = (lax.broadcasted_iota(jnp.int32, (16, plane), 0) % 8).astype(F32)
    strength = count / (1.0 + (k0 * k0 + k1 * k1 + k2 * k2) / 16.0)

    cosine, sine = plane_phases(position)
    cosine, sine = cosine.T, sine.T
    for m in range(orders):
        even = strength[m : m + 1]
        left_ref[m, :, :plane] = (cosine * even).astype(BF)
        left_ref[m, :, plane:] = (sine * even).astype(BF)
        if m:
            odd = strength[8 + m : 9 + m]
            left_ref[reach + m, :, :plane] = (sine * -odd).astype(BF)
            left_ref[reach + m, :, plane:] = (cosine * odd).astype(BF)
    zc, zs = turn_trig(position[2:3])
    zc_ref[...] = jnp.broadcast_to(zc, (rows, rows)).T
    zs_ref[...] = jnp.broadcast_to(zs, (rows, rows)).T


def prepare(wave_index, position, own):
    rows = position.shape[1]
    shapes = (
        jax.ShapeDtypeStruct((rows + extra_rows, own.shape[1]), BF),
        jax.ShapeDtypeStruct((2 * reach + 1, rows, 2 * plane), BF),
        jax.ShapeDtypeStruct((rows, rows), F32),
        jax.ShapeDtypeStruct((rows, rows), F32),
    )
    inputs = (wave_index, position, own)
    return pl.pallas_call(
        prepare_kernel,
        out_shape=shapes,
        grid=(1,),
        in_specs=[whole(x) for x in inputs],
        out_specs=tuple(whole(x) for x in shapes),
        compiler_params=limit,
        name="prepare",
    )(*[in_hbm(x) for x in inputs])


def coupling_kernel(places, rows, left_ref, zc_ref, zs_ref, *refs):
    count = max(p[0] for p in places) + 1
    packed, out_ref, right_ref, part_ref = refs[:count], refs[count], refs[count + 1], refs[count + 2]
    tile = 32
    for pair in range(0, len(places), 2):
        span = min(2, len(places) - pair)
        heights = []
        for side in range(span):
            which, start = places[pair + side]
            block = packed[which][start + rows : start + rows + extra_rows, :].astype(F32)
            position = (block[0:3, :rows] + block[0:3, rows : 2 * rows]) + block[3:6, :rows]
            cosine, sine = plane_phases(position)
            at = slice(side * rows, (side + 1) * rows)
            right_ref[:plane, at] = cosine.astype(BF)
            right_ref[plane:, at] = sine.astype(BF)
            heights.append(turn_trig(position[2:3]))
        wide = span * rows
        for m in range(2 * reach + 1):
            part_ref[m, :, :wide] = dot(left_ref[m], right_ref[:, :wide])
        for side in range(span):
            zc, zs = heights[side]
            at = slice(side * rows, (side + 1) * rows)
            for top in range(0, rows, tile):
                own = slice(top, top + tile)
                oc, os = zc_ref[own, :], zs_ref[own, :]
                c1 = oc * zc + os * zs
                s1 = os * zc - oc * zs
                twice = c1 + c1
                total = part_ref[0, own, at] + c1 * part_ref[1, own, at] + s1 * part_ref[reach + 1, own, at]
                c0, s0 = jnp.ones_like(c1), jnp.zeros_like(s1)
                for m in range(2, orders):
                    c0, c1 = c1, twice * c1 - c0
                    s0, s1 = s1, twice * s1 - s0
                    total = total + c1 * part_ref[m, own, at] + s1 * part_ref[reach + m, own, at]
                out_ref[own, pair * rows + side * rows : pair * rows + (side + 1) * rows] = total.astype(BF)


def coupling(prepared, arrays, places, rows):
    left, zc, zs = prepared
    return pl.pallas_call(
        functools.partial(coupling_kernel, tuple(places), rows),
        out_shape=jax.ShapeDtypeStruct((rows, len(places) * rows), BF),
        scratch_shapes=[
            pltpu.VMEM((2 * plane, 2 * rows), BF),
            pltpu.VMEM((2 * reach + 1, rows, 2 * rows), F32),
        ],
        in_specs=[pl.BlockSpec(memory_space=pltpu.VMEM)] * (3 + len(arrays)),
        out_specs=pl.BlockSpec(memory_space=pltpu.VMEM),
        name="coupling",
        compiler_params=limit,
    )(left, zc, zs, *arrays)


def coupling_of(prepared, arrays, places, blocks, rows):
    used = sorted({places[q][0] for q in blocks})
    spots = [(used.index(places[q][0]), places[q][1]) for q in blocks]
    return coupling(prepared, [arrays[n] for n in used], spots, rows)


def filter_kernel(distance_ref, rbf_ref, filter_ref, out_ref, mark_ref):
    group, rows = distance_ref.shape
    count = rbf_ref.shape[0]
    step = lax.broadcasted_iota(jnp.int32, (count, rows), 0).astype(F32)
    centers = 0.5 + 4.5 * step / (count - 1)
    pieces = []
    for s in range(group):
        offset = distance_ref[s : s + 1, :] - centers
        pieces.append(jnp.exp(-4.0 * offset * offset).astype(BF))
    basis = jnp.concatenate(pieces, axis=1)
    half = dot_dims(basis, rbf_ref[...] * jnp.asarray(0.5, BF), 0, 0)
    inner = (half + half * jnp.tanh(half)).astype(BF)
    out_ref[...] = dot(inner, filter_ref[...]).astype(BF).reshape(out_ref.shape)
    mark_ref[...] = jnp.zeros_like(mark_ref)


def filters_of(distances, w_rbf, w_filter, layer, begin, count):
    slots, rows = distances.shape
    width = w_filter.shape[2]
    return pl.pallas_call(
        filter_kernel,
        out_shape=(
            jax.ShapeDtypeStruct((count * filter_group, rows, width), BF),
            jax.ShapeDtypeStruct((8, 128), F32),
        ),
        grid=(count,),
        in_specs=[
            pl.BlockSpec((filter_group, rows), lambda g: (begin + g, 0)),
            pl.BlockSpec((None,) + w_rbf.shape[1:], lambda g: (layer, 0, 0)),
            pl.BlockSpec((None,) + w_filter.shape[1:], lambda g: (layer, 0, 0)),
        ],
        out_specs=(
            pl.BlockSpec((filter_group, rows, width), lambda g: (g, 0, 0)),
            pl.BlockSpec((8, 128), lambda g: (0, 0)),
        ),
        compiler_params=limit,
        name="filters",
    )(distances, w_rbf, w_filter)


def message_kernel(index_ref, distance_ref, mask_ref, table_ref, *refs):
    filter_refs, out_ref, total_ref = refs[:-2], refs[-2], refs[-1]
    slots, rows = index_ref.shape
    reachable, width = table_ref.shape
    group = message_group
    lane = lax.broadcasted_iota(jnp.int32, (rows, reachable), 1)
    total = jnp.zeros((rows, width), F32)
    per = slots // len(filter_refs)
    for begin in range(0, slots, group):
        at = slice(begin, begin + group)
        index = index_ref[at, :].astype(F32).T.astype(jnp.int32)
        cosine, _ = turn_trig(distance_ref[at, :] * 0.1)
        weight = (0.5 * (cosine + 1.0) * mask_ref[at, :].astype(F32)).T
        picks = [
            jnp.where(lane == index[:, s : s + 1], weight[:, s : s + 1], 0.0).astype(BF)
            for s in range(group)
        ]
        gathered = dot(jnp.concatenate(picks, axis=0), table_ref[...]).reshape(group, rows, width)
        where = begin % per
        factors = filter_refs[begin // per][where : where + group].astype(F32)
        total = total + jnp.sum(gathered * factors, axis=0)
    out_ref[...] = total.astype(BF)


def messages(neighbours, distances, edge_mask, table, filters):
    rows = neighbours.shape[1]
    width = table.shape[1]
    inputs = (neighbours, distances, edge_mask, table) + tuple(filters)
    return pl.pallas_call(
        message_kernel,
        out_shape=jax.ShapeDtypeStruct((rows, width), BF),
        grid=(1,),
        in_specs=[whole(x) for x in inputs],
        out_specs=pl.BlockSpec((rows, width), lambda g: (0, 0)),
        scratch_shapes=[pltpu.VMEM((rows, width), F32)],
        compiler_params=limit,
        name="messages",
    )(*inputs)


def update_kernel(places, before, after, own_ref, message_ref, mixing_ref, short_ref, long_ref, *refs):
    rows, width = own_ref.shape
    counts = sorted({p[0] for p in places})
    pairs = len({p[2] for p in places})
    matrices, states, out_ref = refs[:pairs], refs[pairs : pairs + len(counts)], refs[-1]
    total = jnp.zeros((rows, width), F32)
    for which, start, matrix, column in places:
        total = total + dot(
            matrices[matrix][:, column * rows : (column + 1) * rows], states[which][start : start + rows, :]
        )
    potential = dot((total * before).astype(BF), mixing_ref[...]).astype(BF)
    field = (potential.astype(F32) * after).astype(BF)
    half = 0.5 * (dot(message_ref[...], short_ref[...]) + dot(field, long_ref[...]))
    out_ref[...] = (own_ref[...].astype(F32) + (half + half * jnp.tanh(half))).astype(BF)


def update(own, message, weights, layer, matrices, arrays, places, before, after):
    rows, width = own.shape
    square = pl.BlockSpec((None, width, width), lambda i: (layer, 0, 0))
    return pl.pallas_call(
        functools.partial(update_kernel, tuple(places), before, after),
        out_shape=jax.ShapeDtypeStruct((rows, width), BF),
        grid=(1,),
        in_specs=[whole(own), whole(message), square, square, square]
        + [whole(m) for m in matrices]
        + [whole(a) for a in arrays],
        out_specs=pl.BlockSpec((rows, width), lambda i: (0, 0)),
        name="update",
        compiler_params=limit,
    )(own, message, *weights, *matrices, *arrays)


def swap(x, mask):
    count = lax.axis_size("atom")
    return lax.ppermute(x, "atom", [(i, i ^ mask) for i in range(count)])


def schedule(count):
    bits = [1 << n for n in range(count.bit_length() - 1)][::-1]
    stages, have = [], [0]
    if len(bits) >= 4:
        far, near, side, last = bits[0], bits[1], bits[2], bits[-1]
        first = [far + near, far, near, side]
        stages.append([(mask, [0]) for mask in first + [last]])
        stages.append([(side, first[:3]), (last, first)])
        stages.append([(last, [side + mask for mask in first[:3]])])
        have = [0] + first + [side + mask for mask in first[:3]]
        have = have + [q ^ last for q in have]
        bits = bits[3:-1]
    for bit in bits:
        stages.append([(bit, list(have))])
        have = have + [q ^ bit for q in have]
    return stages


def exchange(arrays, places, stage, size, after=()):
    arrays, places = list(arrays), dict(places)
    sends = []
    for mask, wanted in stage:
        parts = [
            lax.slice_in_dim(arrays[places[q][0]], places[q][1], places[q][1] + size, axis=0)
            for q in wanted
        ]
        sends.append(parts[0] if len(parts) == 1 else jnp.concatenate(parts, axis=0))
    if after:
        sends, after = lax.optimization_barrier((tuple(sends), tuple(after)))
    fresh = {}
    for (mask, wanted), sent in zip(stage, sends):
        arrays.append(swap(sent, mask))
        for n, q in enumerate(wanted):
            fresh[q ^ mask] = (len(arrays) - 1, n * size)
    places.update(fresh)
    return arrays, places, after


def neighbour_table(own, close, even):
    count = lax.axis_size("atom")
    far = lax.ppermute(
        own, "atom", [(i, (i + (count - 1 if i % 2 == 0 else 1)) % count) for i in range(count)]
    )
    return jnp.concatenate([jnp.where(even, far, close), own, jnp.where(even, close, far)], axis=0)


def per_device(
    features,
    fractional,
    distances,
    neighbours,
    edge_mask,
    wave_index,
    w_rbf,
    w_filter,
    w_mixing,
    w_short,
    w_long,
):
    rows, width = features.shape
    slots = neighbours.shape[0]
    bricks = lax.axis_size("atom")
    before = 1.0 / math.sqrt(rows * bricks)
    after = 4.0 / math.sqrt(wave_index.shape[1])
    even = lax.axis_index("atom") % 2 == 0
    stages = schedule(bricks)

    packed, *prepared = prepare(wave_index, fractional, features)
    groups = slots // filter_group
    state = features
    matrices, order = [], []
    for layer in range(w_rbf.shape[0]):
        block = state if layer else packed
        size = block.shape[0]
        arrays, places, _ = exchange([block], {0: (0, 0)}, stages[0], size)
        close = arrays[places[1][0]][:rows] if 1 in places else swap(state, 1)
        table = neighbour_table(state, close, even)
        if layer:
            marked, _ = lax.optimization_barrier((distances, state))
            filters, mark = filters_of(marked, w_rbf, w_filter, layer, 0, groups // 2)
            parts = [filters]
        else:
            filters, mark = filters_of(
                in_hbm(distances), in_hbm(w_rbf), in_hbm(w_filter), layer, 0, groups
            )
            parts = [filters]
        for number, stage in enumerate(stages[1:]):
            old_arrays, old_places = arrays, places
            arrays, places, (mark,) = exchange(arrays, places, stage, size, (mark,))
            if number == 0:
                if layer:
                    marked, mark = lax.optimization_barrier((distances, mark))
                    filters, _ = filters_of(
                        marked, w_rbf, w_filter, layer, groups // 2, groups - groups // 2
                    )
                    parts.append(filters)
                message = messages(neighbours, distances, edge_mask, table, parts)
                mark = message
            else:
                message = mark
            if layer == 0:
                ready = [q for q in old_places if q not in order]
                matrices.append(coupling_of(prepared, old_arrays, old_places, ready, rows))
                order = order + ready
        if layer == 0:
            ready = [q for q in places if q not in order]
            matrices.append(coupling_of(prepared, arrays, places, ready, rows))
            order = order + ready
        spots, at = [], 0
        for number, matrix in enumerate(matrices):
            for column in range(matrix.shape[1] // rows):
                spots.append(places[order[at]] + (number, column))
                at += 1
        state = update(
            state, message, (w_mixing, w_short, w_long), layer, matrices, arrays, spots, before, after
        )
    return state


def solution(mesh):
    along = P(None, ("rep", "atom"))
    in_specs = (P(("rep", "atom"), None), along, along, along, along) + (P(),) * 6
    return jax.shard_map(
        per_device, mesh=mesh, in_specs=in_specs, out_specs=P(("rep", "atom"), None), check_vma=False
    )
```

```python
import functools
import math

import jax
import jax.numpy as jnp
from jax import lax
from jax.experimental import pallas as pl
from jax.experimental.pallas import tpu as pltpu
from jax.sharding import PartitionSpec as P


message_group = 16
reach = 6
orders = reach + 1
columns = 16
plane = (reach + 2) * columns
extra_rows = 16
limit = pltpu.CompilerParams(vmem_limit_bytes=20 << 20)
BF = jnp.bfloat16
F32 = jnp.float32


def dot(a, b):
    return jnp.dot(a, b, preferred_element_type=F32)


def dot_dims(a, b, ca, cb):
    return lax.dot_general(a, b, (((ca,), (cb,)), ((), ())), preferred_element_type=F32)


def turn_trig(turns):
    part = turns - jnp.round(turns)
    angle = part * (2.0 * math.pi)
    square = angle * angle
    cosine = jnp.full_like(square, 1.0 / math.factorial(20))
    for n in range(18, -2, -2):
        cosine = cosine * -square + 1.0 / math.factorial(n)
    sine = jnp.full_like(square, 1.0 / math.factorial(21))
    for n in range(19, -1, -2):
        sine = sine * -square + 1.0 / math.factorial(n)
    return cosine, sine * angle


def plane_phases(position):
    rows = position.shape[1]
    x, y = position[0:1], position[1:2]
    first = lax.broadcasted_iota(jnp.int32, (8, rows), 0).astype(F32)
    second = lax.broadcasted_iota(jnp.int32, (columns, rows), 0).astype(F32) - reach
    xc, xs = turn_trig(first * x)
    yc, ys = turn_trig(second * y)
    cosines, sines = [], []
    for a in range(plane // columns):
        pc, ps = xc[a : a + 1], xs[a : a + 1]
        cosines.append(pc * yc - ps * ys)
        sines.append(pc * ys + ps * yc)
    return jnp.concatenate(cosines, axis=0), jnp.concatenate(sines, axis=0)


def in_hbm(x):
    return pltpu.with_memory_space_constraint(x, pltpu.HBM)


VM = pl.BlockSpec(memory_space=pltpu.VMEM)
RAW = pl.BlockSpec(memory_space=pl.ANY)


def whole(x):
    return pl.BlockSpec(x.shape, lambda i: (0,) * len(x.shape))


def prepare_kernel(wave_ref, position_ref, own_ref, packed_ref, left_ref, zc_ref, zs_ref):
    rows = position_ref.shape[1]
    position = position_ref[...]
    top = position.astype(BF)
    rest = position - top.astype(F32)
    middle = rest.astype(BF)
    low = (rest - middle.astype(F32)).astype(BF)
    blank = jnp.zeros((extra_rows, 2 * rows), BF)
    packed_ref[:rows, :] = own_ref[...]
    packed_ref[rows:, :] = blank
    packed_ref[rows : rows + 3, :rows] = top
    packed_ref[rows : rows + 3, rows : 2 * rows] = middle
    packed_ref[rows + 3 : rows + 6, :rows] = low

    waves = wave_ref.shape[1]
    m0, m1, m2 = wave_ref[0:1, :], wave_ref[1:2, :], wave_ref[2:3, :]
    flip = jnp.logical_or(m0 < 0, jnp.logical_and(m0 == 0, m1 < 0))
    sign = jnp.where(flip, -1, 1)
    code = m0 * sign * columns + m1 * sign + reach
    height = m2 * sign
    row = lax.broadcasted_iota(jnp.int32, (plane, waves), 0)
    chosen = jnp.where(row == code, 1.0, 0.0).astype(BF)
    order = lax.broadcasted_iota(jnp.int32, (16, waves), 0)
    weight = jnp.where(order < 8, 1, jnp.where(height < 0, -1, 1)).astype(F32)
    picked = jnp.where(jnp.abs(height) == order % 8, weight, 0.0).astype(BF)
    count = dot_dims(picked, chosen, 1, 1)
    lane = lax.broadcasted_iota(jnp.int32, (16, plane), 1)
    k0 = (lane // columns).astype(F32)
    k1 = (lane % columns - reach).astype(F32)
    k2 = (lax.broadcasted_iota(jnp.int32, (16, plane), 0) % 8).astype(F32)
    strength = count / (1.0 + (k0 * k0 + k1 * k1 + k2 * k2) / 16.0)

    cosine, sine = plane_phases(position)
    cosine, sine = cosine.T, sine.T
    for m in range(orders):
        even = strength[m : m + 1]
        left_ref[m, :, :plane] = (cosine * even).astype(BF)
        left_ref[m, :, plane:] = (sine * even).astype(BF)
        if m:
            odd = strength[8 + m : 9 + m]
            left_ref[reach + m, :, :plane] = (sine * -odd).astype(BF)
            left_ref[reach + m, :, plane:] = (cosine * odd).astype(BF)
    zc, zs = turn_trig(position[2:3])
    zc_ref[...] = jnp.broadcast_to(zc, (rows, rows)).T
    zs_ref[...] = jnp.broadcast_to(zs, (rows, rows)).T


def prepare(wave_index, position, own):
    rows = position.shape[1]
    shapes = (
        jax.ShapeDtypeStruct((rows + extra_rows, own.shape[1]), BF),
        jax.ShapeDtypeStruct((2 * reach + 1, rows, 2 * plane), BF),
        jax.ShapeDtypeStruct((rows, rows), F32),
        jax.ShapeDtypeStruct((rows, rows), F32),
    )
    inputs = (wave_index, position, own)
    return pl.pallas_call(
        prepare_kernel,
        out_shape=shapes,
        grid=(1,),
        in_specs=[whole(x) for x in inputs],
        out_specs=tuple(whole(x) for x in shapes),
        compiler_params=limit,
        name="prepare",
    )(*[in_hbm(x) for x in inputs])


def coupling_kernel(places, rows, left_ref, zc_ref, zs_ref, *refs):
    count = max(p[0] for p in places) + 1
    packed, out_ref, right_ref, part_ref = refs[:count], refs[count], refs[count + 1], refs[count + 2]
    tile = 32
    for pair in range(0, len(places), 2):
        span = min(2, len(places) - pair)
        heights = []
        for side in range(span):
            which, start = places[pair + side]
            block = packed[which][start + rows : start + rows + extra_rows, :].astype(F32)
            position = (block[0:3, :rows] + block[0:3, rows : 2 * rows]) + block[3:6, :rows]
            cosine, sine = plane_phases(position)
            at = slice(side * rows, (side + 1) * rows)
            right_ref[:plane, at] = cosine.astype(BF)
            right_ref[plane:, at] = sine.astype(BF)
            heights.append(turn_trig(position[2:3]))
        wide = span * rows
        for m in range(2 * reach + 1):
            part_ref[m, :, :wide] = dot(left_ref[m], right_ref[:, :wide])
        for side in range(span):
            zc, zs = heights[side]
            at = slice(side * rows, (side + 1) * rows)
            for top in range(0, rows, tile):
                own = slice(top, top + tile)
                oc, os = zc_ref[own, :], zs_ref[own, :]
                c1 = oc * zc + os * zs
                s1 = os * zc - oc * zs
                twice = c1 + c1
                total = part_ref[0, own, at] + c1 * part_ref[1, own, at] + s1 * part_ref[reach + 1, own, at]
                c0, s0 = jnp.ones_like(c1), jnp.zeros_like(s1)
                for m in range(2, orders):
                    c0, c1 = c1, twice * c1 - c0
                    s0, s1 = s1, twice * s1 - s0
                    total = total + c1 * part_ref[m, own, at] + s1 * part_ref[reach + m, own, at]
                out_ref[own, pair * rows + side * rows : pair * rows + (side + 1) * rows] = total.astype(BF)


def coupling(prepared, arrays, places, rows):
    left, zc, zs = prepared
    return pl.pallas_call(
        functools.partial(coupling_kernel, tuple(places), rows),
        out_shape=jax.ShapeDtypeStruct((rows, len(places) * rows), BF),
        scratch_shapes=[
            pltpu.VMEM((2 * plane, 2 * rows), BF),
            pltpu.VMEM((2 * reach + 1, rows, 2 * rows), F32),
        ],
        in_specs=[pl.BlockSpec(memory_space=pltpu.VMEM)] * (3 + len(arrays)),
        out_specs=pl.BlockSpec(memory_space=pltpu.VMEM),
        name="coupling",
        compiler_params=limit,
    )(left, zc, zs, *arrays)


def coupling_of(prepared, arrays, places, blocks, rows):
    used = sorted({places[q][0] for q in blocks})
    spots = [(used.index(places[q][0]), places[q][1]) for q in blocks]
    return coupling(prepared, [arrays[n] for n in used], spots, rows)


def filter_kernel(layer, begin, fetch, distance_ref, rbf_ref, filter_ref, out_ref, *scratch):
    group, rows, _ = out_ref.shape
    at = slice(begin, begin + group)
    copies = []
    if fetch:
        sources = (distance_ref.at[at], rbf_ref.at[layer], filter_ref.at[layer])
        copies = [
            pltpu.make_async_copy(source, target, scratch[3].at[n])
            for n, (source, target) in enumerate(zip(sources, scratch))
        ]
        for copy in copies:
            copy.start()
        copies[0].wait()
        distance = scratch[0][...]
    else:
        distance = distance_ref[at, :]
    count = rbf_ref.shape[1]
    step = lax.broadcasted_iota(jnp.int32, (count, rows), 0).astype(F32)
    centers = 0.5 + 4.5 * step / (count - 1)
    pieces = []
    for s in range(group):
        offset = distance[s : s + 1, :] - centers
        pieces.append(jnp.exp(-4.0 * offset * offset).astype(BF))
    basis = jnp.concatenate(pieces, axis=1)
    if fetch:
        copies[1].wait()
    first = scratch[1][...] if fetch else rbf_ref[layer]
    half = dot_dims(basis, first * jnp.asarray(0.5, BF), 0, 0)
    inner = (half + half * jnp.tanh(half)).astype(BF)
    if fetch:
        copies[2].wait()
    second = scratch[2][...] if fetch else filter_ref[layer]
    out_ref[...] = dot(inner, second).astype(BF).reshape(out_ref.shape)


def filters_of(distances, w_rbf, w_filter, layer, begin, count, fetch):
    rows = distances.shape[1]
    width = w_filter.shape[2]
    inputs = (distances, w_rbf, w_filter)
    if fetch:
        inputs = tuple(in_hbm(x) for x in inputs)
        scratch = [
            pltpu.VMEM((count, rows), F32),
            pltpu.VMEM(w_rbf.shape[1:], BF),
            pltpu.VMEM(w_filter.shape[1:], BF),
            pltpu.SemaphoreType.DMA((3,)),
        ]
    else:
        scratch = []
    return pl.pallas_call(
        functools.partial(filter_kernel, layer, begin, fetch),
        out_shape=jax.ShapeDtypeStruct((count, rows, width), BF),
        in_specs=[RAW if fetch else VM] * 3,
        out_specs=VM,
        scratch_shapes=scratch,
        compiler_params=limit,
        name="filters",
    )(*inputs)


def message_kernel(index_ref, distance_ref, mask_ref, table_ref, *refs):
    filter_refs, out_ref = refs[:-1], refs[-1]
    slots, rows = index_ref.shape
    reachable, width = table_ref.shape
    group = message_group
    lane = lax.broadcasted_iota(jnp.int32, (rows, reachable), 1)
    total = jnp.zeros((rows, width), F32)
    per = slots // len(filter_refs)
    for begin in range(0, slots, group):
        at = slice(begin, begin + group)
        index = index_ref[at, :].astype(F32).T.astype(jnp.int32)
        cosine, _ = turn_trig(distance_ref[at, :] * 0.1)
        weight = (0.5 * (cosine + 1.0) * mask_ref[at, :].astype(F32)).T
        picks = [
            jnp.where(lane == index[:, s : s + 1], weight[:, s : s + 1], 0.0).astype(BF)
            for s in range(group)
        ]
        gathered = dot(jnp.concatenate(picks, axis=0), table_ref[...]).reshape(group, rows, width)
        where = begin % per
        factors = filter_refs[begin // per][where : where + group].astype(F32)
        total = total + jnp.sum(gathered * factors, axis=0)
    out_ref[...] = total.astype(BF)


def messages(neighbours, distances, edge_mask, table, filters):
    rows = neighbours.shape[1]
    width = table.shape[1]
    inputs = (neighbours, distances, edge_mask, table) + tuple(filters)
    return pl.pallas_call(
        message_kernel,
        out_shape=jax.ShapeDtypeStruct((rows, width), BF),
        in_specs=[VM] * len(inputs),
        out_specs=VM,
        compiler_params=limit,
        name="messages",
    )(*inputs)


def update_kernel(places, layer, before, after, own_ref, message_ref, mixing_ref, short_ref, long_ref, *refs):
    rows, width = own_ref.shape
    counts = sorted({p[0] for p in places})
    pairs = len({p[2] for p in places})
    matrices, states, out_ref = refs[:pairs], refs[pairs : pairs + len(counts)], refs[-1]
    total = jnp.zeros((rows, width), F32)
    for which, start, matrix, column in places:
        total = total + dot(
            matrices[matrix][:, column * rows : (column + 1) * rows], states[which][start : start + rows, :]
        )
    potential = dot((total * before).astype(BF), mixing_ref[layer]).astype(BF)
    field = (potential.astype(F32) * after).astype(BF)
    half = 0.5 * (dot(message_ref[...], short_ref[layer]) + dot(field, long_ref[layer]))
    out_ref[...] = (own_ref[...].astype(F32) + (half + half * jnp.tanh(half))).astype(BF)


def update(own, message, weights, layer, matrices, arrays, places, before, after):
    rows, width = own.shape
    return pl.pallas_call(
        functools.partial(update_kernel, tuple(places), layer, before, after),
        out_shape=jax.ShapeDtypeStruct((rows, width), BF),
        in_specs=[VM] * (5 + len(matrices) + len(arrays)),
        out_specs=VM,
        compiler_params=limit,
        name="update",
    )(own, message, *weights, *matrices, *arrays)


def swap(x, mask):
    count = lax.axis_size("atom")
    return lax.ppermute(x, "atom", [(i, i ^ mask) for i in range(count)])


def schedule(count):
    bits = [1 << n for n in range(count.bit_length() - 1)][::-1]
    stages, have = [], [0]
    if len(bits) >= 4:
        far, near, side, last = bits[0], bits[1], bits[2], bits[-1]
        first = [far + near, far, near, side]
        stages.append([(mask, [0]) for mask in first + [last]])
        stages.append([(side, first[:3]), (last, first)])
        stages.append([(last, [side + mask for mask in first[:3]])])
        have = [0] + first + [side + mask for mask in first[:3]]
        have = have + [q ^ last for q in have]
        bits = bits[3:-1]
    for bit in bits:
        stages.append([(bit, list(have))])
        have = have + [q ^ bit for q in have]
    return stages


def exchange(arrays, places, stage, size):
    arrays, places = list(arrays), dict(places)
    sends = []
    for mask, wanted in stage:
        parts = [
            lax.slice_in_dim(arrays[places[q][0]], places[q][1], places[q][1] + size, axis=0)
            for q in wanted
        ]
        sends.append(parts[0] if len(parts) == 1 else jnp.concatenate(parts, axis=0))
    fresh = {}
    for (mask, wanted), sent in zip(stage, sends):
        arrays.append(swap(sent, mask))
        for n, q in enumerate(wanted):
            fresh[q ^ mask] = (len(arrays) - 1, n * size)
    places.update(fresh)
    return arrays, places


def neighbour_table(own, close, even):
    count = lax.axis_size("atom")
    far = lax.ppermute(
        own, "atom", [(i, (i + (count - 1 if i % 2 == 0 else 1)) % count) for i in range(count)]
    )
    return jnp.concatenate([jnp.where(even, far, close), own, jnp.where(even, close, far)], axis=0)


def per_device(
    features,
    fractional,
    distances,
    neighbours,
    edge_mask,
    wave_index,
    w_rbf,
    w_filter,
    w_mixing,
    w_short,
    w_long,
):
    rows, _ = features.shape
    slots = neighbours.shape[0]
    bricks = lax.axis_size("atom")
    before = 1.0 / math.sqrt(rows * bricks)
    after = 4.0 / math.sqrt(wave_index.shape[1])
    even = lax.axis_index("atom") % 2 == 0
    stages = schedule(bricks)

    packed, *prepared = prepare(wave_index, fractional, features)
    split = slots // 2
    state = features
    matrices, order = [], []

    def couple(arrays, places):
        ready = [q for q in places if q not in order]
        matrices.append(coupling_of(prepared, arrays, places, ready, rows))
        order.extend(ready)

    for layer in range(w_rbf.shape[0]):
        block = state if layer else packed
        size = block.shape[0]
        arrays, places = exchange([block], {0: (0, 0)}, stages[0], size)
        close = arrays[places[1][0]][:rows] if 1 in places else swap(state, 1)
        table = neighbour_table(state, close, even)
        first = filters_of(distances, w_rbf, w_filter, layer, 0, split, layer == 0)
        second = filters_of(distances, w_rbf, w_filter, layer, split, slots - split, False)
        message = messages(neighbours, distances, edge_mask, table, (first, second))
        for stage in stages[1:]:
            if layer == 0:
                couple(arrays, places)
            arrays, places = exchange(arrays, places, stage, size)
        if layer == 0:
            couple(arrays, places)
        spots, at = [], 0
        for number, matrix in enumerate(matrices):
            for column in range(matrix.shape[1] // rows):
                spots.append(places[order[at]] + (number, column))
                at += 1
        weights = (w_mixing, w_short, w_long)
        state = update(
            state, message, weights, layer, matrices, arrays, spots, before, after
        )
    return state


def solution(mesh):
    along = P(None, ("rep", "atom"))
    in_specs = (P(("rep", "atom"), None), along, along, along, along) + (P(),) * 6
    return jax.shard_map(
        per_device, mesh=mesh, in_specs=in_specs, out_specs=P(("rep", "atom"), None), check_vma=False
    )
```

```python
import functools
import math

import jax
import jax.numpy as jnp
from jax import lax
from jax.experimental import pallas as pl
from jax.experimental.pallas import tpu as pltpu
from jax.sharding import PartitionSpec as P


message_group = 16
reach = 6
orders = reach + 1
columns = 16
plane = (reach + 2) * columns
extra_rows = 16
limit = pltpu.CompilerParams(vmem_limit_bytes=20 << 20)
BF = jnp.bfloat16
F32 = jnp.float32


def dot(a, b):
    return jnp.dot(a, b, preferred_element_type=F32)


def dot_dims(a, b, ca, cb):
    return lax.dot_general(a, b, (((ca,), (cb,)), ((), ())), preferred_element_type=F32)


def turn_trig(turns):
    part = turns - jnp.round(turns)
    angle = part * (2.0 * math.pi)
    square = angle * angle
    cosine = jnp.full_like(square, 1.0 / math.factorial(18))
    for n in range(16, -2, -2):
        cosine = cosine * -square + 1.0 / math.factorial(n)
    sine = jnp.full_like(square, 1.0 / math.factorial(19))
    for n in range(17, -1, -2):
        sine = sine * -square + 1.0 / math.factorial(n)
    return cosine, sine * angle


def plane_phases(position):
    rows = position.shape[1]
    x, y = position[0:1], position[1:2]
    first = lax.broadcasted_iota(jnp.int32, (8, rows), 0).astype(F32)
    second = lax.broadcasted_iota(jnp.int32, (columns, rows), 0).astype(F32) - reach
    xc, xs = turn_trig(first * x)
    yc, ys = turn_trig(second * y)
    cosines, sines = [], []
    for a in range(plane // columns):
        pc, ps = xc[a : a + 1], xs[a : a + 1]
        cosines.append(pc * yc - ps * ys)
        sines.append(pc * ys + ps * yc)
    return jnp.concatenate(cosines, axis=0), jnp.concatenate(sines, axis=0)


def in_hbm(x):
    return pltpu.with_memory_space_constraint(x, pltpu.HBM)


VM = pl.BlockSpec(memory_space=pltpu.VMEM)
RAW = pl.BlockSpec(memory_space=pl.ANY)


def whole(x):
    return pl.BlockSpec(x.shape, lambda i: (0,) * len(x.shape))


def prepare_kernel(
    wave_ref, position_ref, own_ref, distance_ref, rbf_ref, filter_ref,
    packed_ref, left_ref, zc_ref, zs_ref, distance_out, rbf_out, filter_out,
):
    distance_out[...] = distance_ref[...]
    rbf_out[...] = rbf_ref[...]
    filter_out[...] = filter_ref[...]
    rows = position_ref.shape[1]
    position = position_ref[...]
    top = position.astype(BF)
    rest = position - top.astype(F32)
    middle = rest.astype(BF)
    low = (rest - middle.astype(F32)).astype(BF)
    blank = jnp.zeros((extra_rows, 2 * rows), BF)
    packed_ref[:rows, :] = own_ref[...]
    packed_ref[rows:, :] = blank
    packed_ref[rows : rows + 3, :rows] = top
    packed_ref[rows : rows + 3, rows : 2 * rows] = middle
    packed_ref[rows + 3 : rows + 6, :rows] = low

    waves = wave_ref.shape[1]
    m0, m1, m2 = wave_ref[0:1, :], wave_ref[1:2, :], wave_ref[2:3, :]
    flip = jnp.logical_or(m0 < 0, jnp.logical_and(m0 == 0, m1 < 0))
    sign = jnp.where(flip, -1, 1)
    code = m0 * sign * columns + m1 * sign + reach
    height = m2 * sign
    row = lax.broadcasted_iota(jnp.int32, (plane, waves), 0)
    chosen = jnp.where(row == code, 1.0, 0.0).astype(BF)
    order = lax.broadcasted_iota(jnp.int32, (16, waves), 0)
    weight = jnp.where(order < 8, 1, jnp.where(height < 0, -1, 1)).astype(F32)
    picked = jnp.where(jnp.abs(height) == order % 8, weight, 0.0).astype(BF)
    count = dot_dims(picked, chosen, 1, 1)
    lane = lax.broadcasted_iota(jnp.int32, (16, plane), 1)
    k0 = (lane // columns).astype(F32)
    k1 = (lane % columns - reach).astype(F32)
    k2 = (lax.broadcasted_iota(jnp.int32, (16, plane), 0) % 8).astype(F32)
    strength = count / (1.0 + (k0 * k0 + k1 * k1 + k2 * k2) / 16.0)

    cosine, sine = plane_phases(position)
    cosine, sine = cosine.T, sine.T
    for m in range(orders):
        even = strength[m : m + 1]
        left_ref[m, :, :plane] = (cosine * even).astype(BF)
        left_ref[m, :, plane:] = (sine * even).astype(BF)
        if m:
            odd = strength[8 + m : 9 + m]
            left_ref[reach + m, :, :plane] = (sine * -odd).astype(BF)
            left_ref[reach + m, :, plane:] = (cosine * odd).astype(BF)
    zc, zs = turn_trig(position[2:3])
    zc_ref[...] = jnp.broadcast_to(zc, (rows, rows)).T
    zs_ref[...] = jnp.broadcast_to(zs, (rows, rows)).T


def prepare(wave_index, position, own, distances, w_rbf, w_filter):
    rows = position.shape[1]
    shapes = (
        jax.ShapeDtypeStruct((rows + extra_rows, own.shape[1]), BF),
        jax.ShapeDtypeStruct((2 * reach + 1, rows, 2 * plane), BF),
        jax.ShapeDtypeStruct((rows, rows), F32),
        jax.ShapeDtypeStruct((rows, rows), F32),
        jax.ShapeDtypeStruct(distances.shape, F32),
        jax.ShapeDtypeStruct((1,) + w_rbf.shape[1:], BF),
        jax.ShapeDtypeStruct((1,) + w_filter.shape[1:], BF),
    )
    inputs = (wave_index, position, own, distances, w_rbf, w_filter)
    return pl.pallas_call(
        prepare_kernel,
        out_shape=shapes,
        grid=(1,),
        in_specs=[whole(x) for x in inputs[:4]] + [whole(x) for x in shapes[-2:]],
        out_specs=(VM,) * len(shapes),
        compiler_params=limit,
        name="prepare",
    )(*[in_hbm(x) for x in inputs])


def coupling_kernel(places, rows, left_ref, zc_ref, zs_ref, *refs):
    count = max(p[0] for p in places) + 1
    packed, out_ref, right_ref, part_ref = refs[:count], refs[count], refs[count + 1], refs[count + 2]
    tile = 32
    for pair in range(0, len(places), 2):
        span = min(2, len(places) - pair)
        heights = []
        for side in range(span):
            which, start = places[pair + side]
            block = packed[which][start + rows : start + rows + extra_rows, :].astype(F32)
            position = (block[0:3, :rows] + block[0:3, rows : 2 * rows]) + block[3:6, :rows]
            cosine, sine = plane_phases(position)
            at = slice(side * rows, (side + 1) * rows)
            right_ref[:plane, at] = cosine.astype(BF)
            right_ref[plane:, at] = sine.astype(BF)
            heights.append(turn_trig(position[2:3]))
        wide = span * rows
        for m in range(2 * reach + 1):
            part_ref[m, :, :wide] = dot(left_ref[m], right_ref[:, :wide])
        for side in range(span):
            zc, zs = heights[side]
            at = slice(side * rows, (side + 1) * rows)
            for top in range(0, rows, tile):
                own = slice(top, top + tile)
                oc, os = zc_ref[own, :], zs_ref[own, :]
                c1 = oc * zc + os * zs
                s1 = os * zc - oc * zs
                twice = c1 + c1
                even, odd = part_ref[reach, own, at], part_ref[2 * reach, own, at]
                even_last, odd_last = 0.0, 0.0
                for m in range(reach - 1, 0, -1):
                    even, even_last = part_ref[m, own, at] + twice * even - even_last, even
                    odd, odd_last = part_ref[reach + m, own, at] + twice * odd - odd_last, odd
                total = part_ref[0, own, at] + c1 * even - even_last + s1 * odd
                out_ref[own, pair * rows + side * rows : pair * rows + (side + 1) * rows] = total.astype(BF)


def coupling(prepared, arrays, places, rows):
    left, zc, zs = prepared
    return pl.pallas_call(
        functools.partial(coupling_kernel, tuple(places), rows),
        out_shape=jax.ShapeDtypeStruct((rows, len(places) * rows), BF),
        scratch_shapes=[
            pltpu.VMEM((2 * plane, 2 * rows), BF),
            pltpu.VMEM((2 * reach + 1, rows, 2 * rows), F32),
        ],
        in_specs=[pl.BlockSpec(memory_space=pltpu.VMEM)] * (3 + len(arrays)),
        out_specs=pl.BlockSpec(memory_space=pltpu.VMEM),
        name="coupling",
        compiler_params=limit,
    )(left, zc, zs, *arrays)


def coupling_of(prepared, arrays, places, blocks, rows):
    used = sorted({places[q][0] for q in blocks})
    spots = [(used.index(places[q][0]), places[q][1]) for q in blocks]
    return coupling(prepared, [arrays[n] for n in used], spots, rows)


def filter_kernel(layer, begin, distance_ref, rbf_ref, filter_ref, out_ref):
    group, rows, _ = out_ref.shape
    count = rbf_ref.shape[1]
    step = lax.broadcasted_iota(jnp.int32, (count, rows), 0).astype(F32)
    centers = 0.5 + 4.5 * step / (count - 1)
    pieces = []
    for s in range(begin, begin + group):
        offset = distance_ref[s : s + 1, :] - centers
        pieces.append(jnp.exp(-4.0 * offset * offset).astype(BF))
    basis = jnp.concatenate(pieces, axis=1)
    half = dot_dims(basis, rbf_ref[layer] * jnp.asarray(0.5, BF), 0, 0)
    inner = (half + half * jnp.tanh(half)).astype(BF)
    out_ref[...] = dot(inner, filter_ref[layer]).astype(BF).reshape(out_ref.shape)


def filters_of(distances, w_rbf, w_filter, layer, begin, count):
    rows = distances.shape[1]
    width = w_filter.shape[2]
    return pl.pallas_call(
        functools.partial(filter_kernel, layer, begin),
        out_shape=jax.ShapeDtypeStruct((count, rows, width), BF),
        in_specs=[VM] * 3,
        out_specs=VM,
        compiler_params=limit,
        name="filters",
    )(distances, w_rbf, w_filter)


def code_of(index):
    return jnp.where(index < 256, index, 255 - index).astype(F32).astype(BF)


def message_kernel(index_ref, distance_ref, mask_ref, table_ref, *refs):
    filter_refs, out_ref = refs[:-1], refs[-1]
    slots, rows = index_ref.shape
    reachable, width = table_ref.shape
    group = message_group
    lane = code_of(lax.broadcasted_iota(jnp.int32, (rows, reachable), 1))
    total = jnp.zeros((rows, width), F32)
    per = slots // len(filter_refs)
    for begin in range(0, slots, group):
        at = slice(begin, begin + group)
        code = code_of(index_ref[at, :]).astype(F32).T.astype(BF)
        cosine, _ = turn_trig(distance_ref[at, :] * 0.1)
        weight = (0.5 * (cosine + 1.0) * mask_ref[at, :].astype(F32)).T.astype(BF)
        picks = [
            jnp.where(lane == code[:, s : s + 1], weight[:, s : s + 1], jnp.zeros((), BF))
            for s in range(group)
        ]
        gathered = dot(jnp.concatenate(picks, axis=0), table_ref[...]).reshape(group, rows, width)
        where = begin % per
        factors = filter_refs[begin // per][where : where + group].astype(F32)
        total = total + jnp.sum(gathered * factors, axis=0)
    out_ref[...] = total.astype(BF)


def messages(neighbours, distances, edge_mask, table, filters):
    rows = neighbours.shape[1]
    width = table.shape[1]
    inputs = (neighbours, distances, edge_mask, table) + tuple(filters)
    return pl.pallas_call(
        message_kernel,
        out_shape=jax.ShapeDtypeStruct((rows, width), BF),
        in_specs=[VM] * len(inputs),
        out_specs=VM,
        compiler_params=limit,
        name="messages",
    )(*inputs)


def gathered_field(places, rows, matrices, states):
    total = None
    for which, start, matrix, column in places:
        part = dot(
            matrices[matrix][:, column * rows : (column + 1) * rows], states[which][start : start + rows, :]
        )
        total = part if total is None else total + part
    return total


def partial_kernel(places, pairs, layer, message_ref, short_ref, *refs):
    matrices, states, total_ref, close_ref = refs[:pairs], refs[pairs:-2], refs[-2], refs[-1]
    total_ref[...] = gathered_field(places, message_ref.shape[0], matrices, states)
    close_ref[...] = dot(message_ref[...], short_ref[layer])


def partial_update(message, w_short, layer, matrices, arrays, places):
    shape = jax.ShapeDtypeStruct(message.shape, F32)
    return pl.pallas_call(
        functools.partial(partial_kernel, tuple(places), len(matrices), layer),
        out_shape=(shape, shape),
        in_specs=[VM] * (2 + len(matrices) + len(arrays)),
        out_specs=(VM, VM),
        compiler_params=limit,
        name="partial",
    )(message, w_short, *matrices, *arrays)


def update_kernel(places, pairs, begun, layer, before, after, own_ref, mixing_ref, long_ref, *refs):
    rows, _ = own_ref.shape
    head, matrices, states, out_ref = refs[:2], refs[2 : 2 + pairs], refs[2 + pairs : -1], refs[-1]
    total = gathered_field(places, rows, matrices, states)
    if begun:
        total = total + head[0][...]
        close = head[1][...]
    else:
        close = dot(head[0][...], head[1][layer])
    potential = dot((total * before).astype(BF), mixing_ref[layer]).astype(BF)
    field = (potential.astype(F32) * after).astype(BF)
    half = 0.5 * (close + dot(field, long_ref[layer]))
    out_ref[...] = (own_ref[...].astype(F32) + (half + half * jnp.tanh(half))).astype(BF)


def update(own, head, begun, mixing, long, layer, matrices, arrays, places, before, after):
    return pl.pallas_call(
        functools.partial(update_kernel, tuple(places), len(matrices), begun, layer, before, after),
        out_shape=jax.ShapeDtypeStruct(own.shape, BF),
        in_specs=[VM] * (5 + len(matrices) + len(arrays)),
        out_specs=VM,
        compiler_params=limit,
        name="update",
    )(own, mixing, long, *head, *matrices, *arrays)


def picked(spots, matrices, arrays):
    rows = sorted({spot[2] for spot in spots})
    used = sorted({spot[0] for spot in spots})
    spots = [(used.index(a), s, rows.index(m), c) for a, s, m, c in spots]
    return [matrices[m] for m in rows], [arrays[a] for a in used], spots


def swap(x, even, odd):
    count = lax.axis_size("atom")
    return lax.ppermute(x, "atom", [(i, i ^ (odd if i % 2 else even)) for i in range(count)])


def schedule(count):
    bits = [1 << n for n in range(count.bit_length() - 1)][::-1]
    stages, have = [], [0]
    if len(bits) >= 4:
        far, near, side, last = bits[0], bits[1], bits[2], bits[-1]
        first = [far + near, far, near]
        second = [side + q for q in first]
        early = first + [side]
        stages.append([(mask, mask, [0], [mask]) for mask in early + [last]])
        stages.append([(side, side, first, second), (last, last, early, [last + q for q in early])])
        stages.append([(last, last, second, [last + q for q in second])])
        have = [0] + [q for stage in stages for item in stage for q in item[3]]
        bits = bits[3:-1]
    for bit in bits:
        stages.append([(bit, bit, list(have), [q ^ bit for q in have])])
        have = have + [q ^ bit for q in have]
    return stages


def exchange(arrays, places, stage, size):
    arrays, places = list(arrays), dict(places)
    sends = []
    for _, _, wanted, _ in stage:
        parts = [
            lax.slice_in_dim(arrays[places[q][0]], places[q][1], places[q][1] + size, axis=0)
            for q in wanted
        ]
        sends.append(parts[0] if len(parts) == 1 else jnp.concatenate(parts, axis=0))
    for (even, odd, _, labels), sent in zip(stage, sends):
        arrays.append(swap(sent, even, odd))
        for n, q in enumerate(labels):
            places[q] = (len(arrays) - 1, n * size)
    return arrays, places


def neighbour_table(own, close, even):
    count = lax.axis_size("atom")
    far = lax.ppermute(
        own, "atom", [(i, (i + (count - 1 if i % 2 == 0 else 1)) % count) for i in range(count)]
    )
    return jnp.concatenate([jnp.where(even, far, close), own, jnp.where(even, close, far)], axis=0)


def per_device(
    features,
    fractional,
    distances,
    neighbours,
    edge_mask,
    wave_index,
    w_rbf,
    w_filter,
    w_mixing,
    w_short,
    w_long,
):
    rows, _ = features.shape
    slots = neighbours.shape[0]
    bricks = lax.axis_size("atom")
    before = 1.0 / math.sqrt(rows * bricks)
    after = 4.0 / math.sqrt(wave_index.shape[1])
    even = lax.axis_index("atom") % 2 == 0
    stages = schedule(bricks)

    packed, *prepared, near_distances, first_rbf, first_filter = prepare(
        wave_index, fractional, features, distances, w_rbf, w_filter
    )
    split = slots // 2
    state = features
    matrices, where = [], {}

    def couple(arrays, places, keep=0):
        ready = [q for q in places if q not in where]
        ready = ready[: len(ready) - keep]
        matrix = coupling_of(prepared, arrays, places, ready, rows)
        where.update({q: (len(matrices), n) for n, q in enumerate(ready)})
        matrices.append(matrix)

    for layer in range(w_rbf.shape[0]):
        block = state if layer else packed
        size = block.shape[0]
        arrays, places = exchange([block], {0: (0, 0)}, stages[0], size)
        close = arrays[places[1][0]][:rows] if 1 in places else swap(state, 1, 1)
        table = neighbour_table(state, close, even)
        if layer:
            edge = (distances, w_rbf, w_filter, layer)
        else:
            edge = (near_distances, first_rbf, first_filter, 0)
        first = filters_of(*edge, 0, split)
        second = filters_of(*edge, split, slots - split)
        message = messages(neighbours, edge[0], edge_mask, table, (first, second))
        for stage in stages[1:]:
            if layer == 0:
                couple(arrays, places)
            early = list(places)
            arrays, places = exchange(arrays, places, stage, size)
        if layer == 0:
            couple(arrays, places)
            early = []
        spot = {q: places[q] + where[q] for q in places}
        head, late = (message, w_short), [q for q in places if q not in early]
        if early:
            used, held, spots = picked([spot[q] for q in early], matrices, arrays)
            head = partial_update(message, w_short, layer, used, held, spots)
        used, held, spots = picked([spot[q] for q in late], matrices, arrays)
        state = update(
            state, head, bool(early), w_mixing, w_long, layer, used, held, spots, before, after
        )
    return state


def solution(mesh):
    along = P(None, ("rep", "atom"))
    in_specs = (P(("rep", "atom"), None), along, along, along, along) + (P(),) * 6
    return jax.shard_map(
        per_device, mesh=mesh, in_specs=in_specs, out_specs=P(("rep", "atom"), None), check_vma=False
    )
```

```python
import functools
import math

import jax
import jax.numpy as jnp
from jax import lax
from jax.experimental import pallas as pl
from jax.experimental.pallas import tpu as pltpu
from jax.sharding import PartitionSpec as P


message_group = 16
filter_group = 8
reach = 6
orders = reach + 1
columns = 16
plane = (reach + 2) * columns
extra_rows = 16
limit = pltpu.CompilerParams(vmem_limit_bytes=20 << 20)
BF = jnp.bfloat16
F32 = jnp.float32


def dot(a, b):
    return jnp.dot(a, b, preferred_element_type=F32)


def dot_dims(a, b, ca, cb):
    return lax.dot_general(a, b, (((ca,), (cb,)), ((), ())), preferred_element_type=F32)


def turn_trig(turns):
    part = turns - jnp.round(turns)
    angle = part * (2.0 * math.pi)
    square = angle * angle
    cosine = jnp.full_like(square, 1.0 / math.factorial(18))
    for n in range(16, -2, -2):
        cosine = cosine * -square + 1.0 / math.factorial(n)
    sine = jnp.full_like(square, 1.0 / math.factorial(19))
    for n in range(17, -1, -2):
        sine = sine * -square + 1.0 / math.factorial(n)
    return cosine, sine * angle


def plane_phases(position):
    rows = position.shape[1]
    x, y = position[0:1], position[1:2]
    first = lax.broadcasted_iota(jnp.int32, (8, rows), 0).astype(F32)
    second = lax.broadcasted_iota(jnp.int32, (columns, rows), 0).astype(F32) - reach
    xc, xs = turn_trig(first * x)
    yc, ys = turn_trig(second * y)
    cosines, sines = [], []
    for a in range(plane // columns):
        pc, ps = xc[a : a + 1], xs[a : a + 1]
        cosines.append(pc * yc - ps * ys)
        sines.append(pc * ys + ps * yc)
    return jnp.concatenate(cosines, axis=0), jnp.concatenate(sines, axis=0)


def in_hbm(x):
    return pltpu.with_memory_space_constraint(x, pltpu.HBM)


VM = pl.BlockSpec(memory_space=pltpu.VMEM)
RAW = pl.BlockSpec(memory_space=pl.ANY)


def whole(x):
    return pl.BlockSpec(x.shape, lambda i: (0,) * len(x.shape))


def prepare_kernel(
    wave_ref, position_ref, own_ref, distance_ref, rbf_ref, filter_ref,
    packed_ref, left_ref, zc_ref, zs_ref, distance_out, rbf_out, filter_out,
):
    distance_out[...] = distance_ref[...]
    rbf_out[...] = rbf_ref[...]
    filter_out[...] = filter_ref[...]
    rows = position_ref.shape[1]
    position = position_ref[...]
    top = position.astype(BF)
    rest = position - top.astype(F32)
    middle = rest.astype(BF)
    low = (rest - middle.astype(F32)).astype(BF)
    blank = jnp.zeros((extra_rows, 2 * rows), BF)
    packed_ref[:rows, :] = own_ref[...]
    packed_ref[rows:, :] = blank
    packed_ref[rows : rows + 3, :rows] = top
    packed_ref[rows : rows + 3, rows : 2 * rows] = middle
    packed_ref[rows + 3 : rows + 6, :rows] = low

    waves = wave_ref.shape[1]
    m0, m1, m2 = wave_ref[0:1, :], wave_ref[1:2, :], wave_ref[2:3, :]
    flip = jnp.logical_or(m0 < 0, jnp.logical_and(m0 == 0, m1 < 0))
    sign = jnp.where(flip, -1, 1)
    code = m0 * sign * columns + m1 * sign + reach
    height = m2 * sign
    row = lax.broadcasted_iota(jnp.int32, (plane, waves), 0)
    chosen = jnp.where(row == code, 1.0, 0.0).astype(BF)
    order = lax.broadcasted_iota(jnp.int32, (16, waves), 0)
    weight = jnp.where(order < 8, 1, jnp.where(height < 0, -1, 1)).astype(F32)
    picked = jnp.where(jnp.abs(height) == order % 8, weight, 0.0).astype(BF)
    count = dot_dims(picked, chosen, 1, 1)
    lane = lax.broadcasted_iota(jnp.int32, (16, plane), 1)
    k0 = (lane // columns).astype(F32)
    k1 = (lane % columns - reach).astype(F32)
    k2 = (lax.broadcasted_iota(jnp.int32, (16, plane), 0) % 8).astype(F32)
    strength = count / (1.0 + (k0 * k0 + k1 * k1 + k2 * k2) / 16.0)

    cosine, sine = plane_phases(position)
    cosine, sine = cosine.T, sine.T
    for m in range(orders):
        even = strength[m : m + 1]
        left_ref[m, :, :plane] = (cosine * even).astype(BF)
        left_ref[m, :, plane:] = (sine * even).astype(BF)
        if m:
            odd = strength[8 + m : 9 + m]
            left_ref[reach + m, :, :plane] = (sine * -odd).astype(BF)
            left_ref[reach + m, :, plane:] = (cosine * odd).astype(BF)
    zc, zs = turn_trig(position[2:3])
    zc_ref[...] = jnp.broadcast_to(zc, (rows, rows)).T
    zs_ref[...] = jnp.broadcast_to(zs, (rows, rows)).T


def prepare(wave_index, position, own, distances, w_rbf, w_filter):
    rows = position.shape[1]
    shapes = (
        jax.ShapeDtypeStruct((rows + extra_rows, own.shape[1]), BF),
        jax.ShapeDtypeStruct((2 * reach + 1, rows, 2 * plane), BF),
        jax.ShapeDtypeStruct((rows, rows), F32),
        jax.ShapeDtypeStruct((rows, rows), F32),
        jax.ShapeDtypeStruct(distances.shape, F32),
        jax.ShapeDtypeStruct((1,) + w_rbf.shape[1:], BF),
        jax.ShapeDtypeStruct((1,) + w_filter.shape[1:], BF),
    )
    inputs = (wave_index, position, own, distances, w_rbf, w_filter)
    return pl.pallas_call(
        prepare_kernel,
        out_shape=shapes,
        grid=(1,),
        in_specs=[whole(x) for x in inputs[:4]] + [whole(x) for x in shapes[-2:]],
        out_specs=(VM,) * len(shapes),
        compiler_params=limit,
        name="prepare",
    )(*[in_hbm(x) for x in inputs])


def coupling_kernel(places, rows, left_ref, zc_ref, zs_ref, *refs):
    count = max(p[0] for p in places) + 1
    packed, out_ref, right_ref, part_ref = refs[:count], refs[count], refs[count + 1], refs[count + 2]
    tile = 32
    for pair in range(0, len(places), 2):
        span = min(2, len(places) - pair)
        heights = []
        for side in range(span):
            which, start = places[pair + side]
            block = packed[which][start + rows : start + rows + extra_rows, :].astype(F32)
            position = (block[0:3, :rows] + block[0:3, rows : 2 * rows]) + block[3:6, :rows]
            cosine, sine = plane_phases(position)
            at = slice(side * rows, (side + 1) * rows)
            right_ref[:plane, at] = cosine.astype(BF)
            right_ref[plane:, at] = sine.astype(BF)
            heights.append(turn_trig(position[2:3]))
        wide = span * rows
        for m in range(2 * reach + 1):
            part_ref[m, :, :wide] = dot(left_ref[m], right_ref[:, :wide])
        for side in range(span):
            zc, zs = heights[side]
            at = slice(side * rows, (side + 1) * rows)
            for top in range(0, rows, tile):
                own = slice(top, top + tile)
                oc, os = zc_ref[own, :], zs_ref[own, :]
                c1 = oc * zc + os * zs
                s1 = os * zc - oc * zs
                twice = c1 + c1
                even, odd = part_ref[reach, own, at], part_ref[2 * reach, own, at]
                even_last, odd_last = 0.0, 0.0
                for m in range(reach - 1, 0, -1):
                    even, even_last = part_ref[m, own, at] + twice * even - even_last, even
                    odd, odd_last = part_ref[reach + m, own, at] + twice * odd - odd_last, odd
                total = part_ref[0, own, at] + c1 * even - even_last + s1 * odd
                out_ref[own, pair * rows + side * rows : pair * rows + (side + 1) * rows] = total.astype(BF)


def coupling(prepared, arrays, places, rows):
    left, zc, zs = prepared
    return pl.pallas_call(
        functools.partial(coupling_kernel, tuple(places), rows),
        out_shape=jax.ShapeDtypeStruct((rows, len(places) * rows), BF),
        scratch_shapes=[
            pltpu.VMEM((2 * plane, 2 * rows), BF),
            pltpu.VMEM((2 * reach + 1, rows, 2 * rows), F32),
        ],
        in_specs=[pl.BlockSpec(memory_space=pltpu.VMEM)] * (3 + len(arrays)),
        out_specs=pl.BlockSpec(memory_space=pltpu.VMEM),
        name="coupling",
        compiler_params=limit,
    )(left, zc, zs, *arrays)


def coupling_of(prepared, arrays, places, blocks, rows):
    used = sorted({places[q][0] for q in blocks})
    spots = [(used.index(places[q][0]), places[q][1]) for q in blocks]
    return coupling(prepared, [arrays[n] for n in used], spots, rows)


def centers_of(count, rows):
    step = lax.broadcasted_iota(jnp.int32, (count, rows), 0).astype(F32)
    return 0.5 + 4.5 * step / (count - 1)


def filters_at(distance_ref, begin, count, centers, first, second):
    pieces = []
    for s in range(begin, begin + count):
        offset = distance_ref[s : s + 1, :] - centers
        pieces.append(jnp.exp(-4.0 * offset * offset).astype(BF))
    half = dot_dims(jnp.concatenate(pieces, axis=1), first, 0, 0)
    inner = (half + half * jnp.tanh(half)).astype(BF)
    return dot(inner, second).reshape(count, centers.shape[1], second.shape[1])


def filter_kernel(layer, distance_ref, rbf_ref, filter_ref, out_ref):
    group, rows, _ = out_ref.shape
    centers = centers_of(rbf_ref.shape[1], rows)
    first = rbf_ref[layer] * jnp.asarray(0.5, BF)
    for chunk in range(0, group, filter_group):
        made = filters_at(distance_ref, chunk, filter_group, centers, first, filter_ref[layer])
        out_ref[chunk : chunk + filter_group] = made.astype(BF)


def filters_of(distances, w_rbf, w_filter, layer, count):
    rows = distances.shape[1]
    width = w_filter.shape[2]
    return pl.pallas_call(
        functools.partial(filter_kernel, layer),
        out_shape=jax.ShapeDtypeStruct((count, rows, width), BF),
        in_specs=[VM] * 3,
        out_specs=VM,
        compiler_params=limit,
        name="filters",
    )(distances, w_rbf, w_filter)


def code_of(index):
    return jnp.where(index < 256, index, 255 - index).astype(F32).astype(BF)


def message_kernel(
    layer, index_ref, distance_ref, mask_ref, table_ref, rbf_ref, filter_ref, ready_ref, out_ref
):
    slots, rows = index_ref.shape
    reachable, width = table_ref.shape
    ready = ready_ref.shape[0]
    lane = code_of(lax.broadcasted_iota(jnp.int32, (rows, reachable), 1))
    centers = centers_of(rbf_ref.shape[1], rows)
    first = rbf_ref[layer] * jnp.asarray(0.5, BF)
    total = jnp.zeros((rows, width), F32)
    group = message_group
    starts = [n for pair in zip(range(0, ready, group), range(ready, slots, group)) for n in pair]
    starts += [n for n in range(0, slots, group) if n not in starts]
    for begin in starts:
        at = slice(begin, begin + group)
        code = code_of(index_ref[at, :]).astype(F32).T.astype(BF)
        cosine, _ = turn_trig(distance_ref[at, :] * 0.1)
        weight = (0.5 * (cosine + 1.0) * mask_ref[at, :].astype(F32)).T.astype(BF)
        picks = [
            jnp.where(lane == code[:, s : s + 1], weight[:, s : s + 1], jnp.zeros((), BF))
            for s in range(group)
        ]
        gathered = dot(jnp.concatenate(picks, axis=0), table_ref[...]).reshape(group, rows, width)
        if begin < ready:
            factors = ready_ref[at].astype(F32)
        else:
            factors = filters_at(distance_ref, begin, group, centers, first, filter_ref[layer])
        total = total + jnp.sum(gathered * factors, axis=0)
    out_ref[...] = total.astype(BF)


def messages(neighbours, distances, edge_mask, table, w_rbf, w_filter, layer, ready):
    inputs = (neighbours, distances, edge_mask, table, w_rbf, w_filter, ready)
    return pl.pallas_call(
        functools.partial(message_kernel, layer),
        out_shape=jax.ShapeDtypeStruct((neighbours.shape[1], table.shape[1]), BF),
        in_specs=[VM] * len(inputs),
        out_specs=VM,
        compiler_params=limit,
        name="messages",
    )(*inputs)


def gathered_field(places, rows, matrices, states):
    total = None
    for which, start, matrix, column in places:
        part = dot(
            matrices[matrix][:, column * rows : (column + 1) * rows], states[which][start : start + rows, :]
        )
        total = part if total is None else total + part
    return total


def partial_kernel(places, pairs, layer, message_ref, short_ref, *refs):
    matrices, states, total_ref, close_ref = refs[:pairs], refs[pairs:-2], refs[-2], refs[-1]
    total_ref[...] = gathered_field(places, message_ref.shape[0], matrices, states)
    close_ref[...] = dot(message_ref[...], short_ref[layer])


def partial_update(message, w_short, layer, matrices, arrays, places):
    shape = jax.ShapeDtypeStruct(message.shape, F32)
    return pl.pallas_call(
        functools.partial(partial_kernel, tuple(places), len(matrices), layer),
        out_shape=(shape, shape),
        in_specs=[VM] * (2 + len(matrices) + len(arrays)),
        out_specs=(VM, VM),
        compiler_params=limit,
        name="partial",
    )(message, w_short, *matrices, *arrays)


def update_kernel(places, pairs, begun, layer, before, after, own_ref, mixing_ref, long_ref, *refs):
    rows, _ = own_ref.shape
    head, matrices, states, out_ref = refs[:2], refs[2 : 2 + pairs], refs[2 + pairs : -1], refs[-1]
    total = gathered_field(places, rows, matrices, states)
    if begun:
        total = total + head[0][...]
        close = head[1][...]
    else:
        close = dot(head[0][...], head[1][layer])
    potential = dot((total * before).astype(BF), mixing_ref[layer]).astype(BF)
    field = (potential.astype(F32) * after).astype(BF)
    half = 0.5 * (close + dot(field, long_ref[layer]))
    out_ref[...] = (own_ref[...].astype(F32) + (half + half * jnp.tanh(half))).astype(BF)


def update(own, head, begun, mixing, long, layer, matrices, arrays, places, before, after):
    return pl.pallas_call(
        functools.partial(update_kernel, tuple(places), len(matrices), begun, layer, before, after),
        out_shape=jax.ShapeDtypeStruct(own.shape, BF),
        in_specs=[VM] * (5 + len(matrices) + len(arrays)),
        out_specs=VM,
        compiler_params=limit,
        name="update",
    )(own, mixing, long, *head, *matrices, *arrays)


def picked(spots, matrices, arrays):
    rows = sorted({spot[2] for spot in spots})
    used = sorted({spot[0] for spot in spots})
    spots = [(used.index(a), s, rows.index(m), c) for a, s, m, c in spots]
    return [matrices[m] for m in rows], [arrays[a] for a in used], spots


def swap(x, even, odd):
    count = lax.axis_size("atom")
    return lax.ppermute(x, "atom", [(i, i ^ (odd if i % 2 else even)) for i in range(count)])


def schedule(count, lean):
    bits = [1 << n for n in range(count.bit_length() - 1)][::-1]
    stages, have = [], [0]
    if len(bits) >= 4:
        far, near, side, last = bits[0], bits[1], bits[2], bits[-1]
        first = [far + near, far, near]
        early = first if lean else first + [side]
        sent = [0] + first if lean else first
        second = [side + q for q in sent]
        stages.append([(mask, mask, [0], [mask]) for mask in early + [last]])
        stages.append([(side, side, sent, second), (last, last, early, [last + q for q in early])])
        stages.append([(last, last, second, [last + q for q in second])])
        have = [0] + [q for stage in stages for item in stage for q in item[3]]
        bits = bits[3:-1]
    for bit in bits:
        stages.append([(bit, bit, list(have), [q ^ bit for q in have])])
        have = have + [q ^ bit for q in have]
    return stages


def exchange(arrays, places, stage, size):
    arrays, places = list(arrays), dict(places)
    sends = []
    for _, _, wanted, _ in stage:
        parts = [
            lax.slice_in_dim(arrays[places[q][0]], places[q][1], places[q][1] + size, axis=0)
            for q in wanted
        ]
        sends.append(parts[0] if len(parts) == 1 else jnp.concatenate(parts, axis=0))
    for (even, odd, _, labels), sent in zip(stage, sends):
        arrays.append(swap(sent, even, odd))
        for n, q in enumerate(labels):
            places[q] = (len(arrays) - 1, n * size)
    return arrays, places


def neighbour_table(own, close, even):
    count = lax.axis_size("atom")
    far = lax.ppermute(
        own, "atom", [(i, (i + (count - 1 if i % 2 == 0 else 1)) % count) for i in range(count)]
    )
    return jnp.concatenate([jnp.where(even, far, close), own, jnp.where(even, close, far)], axis=0)


def per_device(
    features,
    fractional,
    distances,
    neighbours,
    edge_mask,
    wave_index,
    w_rbf,
    w_filter,
    w_mixing,
    w_short,
    w_long,
):
    rows, _ = features.shape
    slots = neighbours.shape[0]
    bricks = lax.axis_size("atom")
    before = 1.0 / math.sqrt(rows * bricks)
    after = 4.0 / math.sqrt(wave_index.shape[1])
    even = lax.axis_index("atom") % 2 == 0

    packed, *prepared, near_distances, first_rbf, first_filter = prepare(
        wave_index, fractional, features, distances, w_rbf, w_filter
    )
    state = features
    matrices, where = [], {}

    def couple(arrays, places):
        ready = [q for q in places if q not in where]
        if len(places) < bricks:
            ready = ready[: len(ready) // 2 * 2]
        matrix = coupling_of(prepared, arrays, places, ready, rows)
        where.update({q: (len(matrices), n) for n, q in enumerate(ready)})
        matrices.append(matrix)

    for layer in range(w_rbf.shape[0]):
        block = state if layer else packed
        stages = schedule(bricks, False)
        size = block.shape[0]
        arrays, places = exchange([block], {0: (0, 0)}, stages[0], size)
        close = arrays[places[1][0]][:rows] if 1 in places else swap(state, 1, 1)
        table = neighbour_table(state, close, even)
        if layer:
            edge = (distances, w_rbf, w_filter, layer)
        else:
            edge = (near_distances, first_rbf, first_filter, 0)
        ready = filters_of(*edge, slots // 2)
        message = messages(neighbours, edge[0], edge_mask, table, *edge[1:], ready)
        for stage in stages[1:]:
            if layer == 0:
                couple(arrays, places)
            early = list(places)
            arrays, places = exchange(arrays, places, stage, size)
        if layer == 0:
            couple(arrays, places)
            early = []
        spot = {q: places[q] + where[q] for q in places}
        head, late = (message, w_short), [q for q in places if q not in early]
        if early:
            used, held, spots = picked([spot[q] for q in early], matrices, arrays)
            head = partial_update(message, w_short, layer, used, held, spots)
        used, held, spots = picked([spot[q] for q in late], matrices, arrays)
        state = update(
            state, head, bool(early), w_mixing, w_long, layer, used, held, spots, before, after
        )
    return state


def solution(mesh):
    along = P(None, ("rep", "atom"))
    in_specs = (P(("rep", "atom"), None), along, along, along, along) + (P(),) * 6
    return jax.shard_map(
        per_device, mesh=mesh, in_specs=in_specs, out_specs=P(("rep", "atom"), None), check_vma=False
    )
```

```python
import functools
import math

import jax
import jax.numpy as jnp
from jax import lax
from jax.experimental import pallas as pl
from jax.experimental.pallas import tpu as pltpu
from jax.sharding import PartitionSpec as P


message_group = 16
filter_group = 8
reach = 6
orders = reach + 1
columns = 16
plane = (reach + 2) * columns
extra_rows = 16
limit = pltpu.CompilerParams(vmem_limit_bytes=20 << 20)
BF = jnp.bfloat16
F32 = jnp.float32


def dot(a, b):
    return jnp.dot(a, b, preferred_element_type=F32)


def dot_dims(a, b, ca, cb):
    return lax.dot_general(a, b, (((ca,), (cb,)), ((), ())), preferred_element_type=F32)


def turn_trig(turns):
    part = turns - jnp.round(turns)
    angle = part * (2.0 * math.pi)
    square = angle * angle
    cosine = jnp.full_like(square, 1.0 / math.factorial(18))
    for n in range(16, -2, -2):
        cosine = cosine * -square + 1.0 / math.factorial(n)
    sine = jnp.full_like(square, 1.0 / math.factorial(19))
    for n in range(17, -1, -2):
        sine = sine * -square + 1.0 / math.factorial(n)
    return cosine, sine * angle


def plane_phases(position):
    rows = position.shape[1]
    x, y = position[0:1], position[1:2]
    first = lax.broadcasted_iota(jnp.int32, (8, rows), 0).astype(F32)
    second = lax.broadcasted_iota(jnp.int32, (columns, rows), 0).astype(F32) - reach
    xc, xs = turn_trig(first * x)
    yc, ys = turn_trig(second * y)
    cosines, sines = [], []
    for a in range(plane // columns):
        pc, ps = xc[a : a + 1], xs[a : a + 1]
        cosines.append(pc * yc - ps * ys)
        sines.append(pc * ys + ps * yc)
    return jnp.concatenate(cosines, axis=0), jnp.concatenate(sines, axis=0)


def in_hbm(x):
    return pltpu.with_memory_space_constraint(x, pltpu.HBM)


VM = pl.BlockSpec(memory_space=pltpu.VMEM)
RAW = pl.BlockSpec(memory_space=pl.ANY)


def whole(x):
    return pl.BlockSpec(x.shape, lambda i: (0,) * len(x.shape))


def prepare_kernel(
    wave_ref, position_ref, own_ref, distance_ref, rbf_ref, filter_ref,
    packed_ref, left_ref, zc_ref, zs_ref, distance_out, rbf_out, filter_out,
):
    distance_out[...] = distance_ref[...]
    rbf_out[...] = rbf_ref[...]
    filter_out[...] = filter_ref[...]
    rows = position_ref.shape[1]
    position = position_ref[...]
    top = position.astype(BF)
    rest = position - top.astype(F32)
    middle = rest.astype(BF)
    low = (rest - middle.astype(F32)).astype(BF)
    blank = jnp.zeros((extra_rows, 2 * rows), BF)
    packed_ref[:rows, :] = own_ref[...]
    packed_ref[rows:, :] = blank
    packed_ref[rows : rows + 3, :rows] = top
    packed_ref[rows : rows + 3, rows : 2 * rows] = middle
    packed_ref[rows + 3 : rows + 6, :rows] = low

    waves = wave_ref.shape[1]
    m0, m1, m2 = wave_ref[0:1, :], wave_ref[1:2, :], wave_ref[2:3, :]
    flip = jnp.logical_or(m0 < 0, jnp.logical_and(m0 == 0, m1 < 0))
    sign = jnp.where(flip, -1, 1)
    code = m0 * sign * columns + m1 * sign + reach
    height = m2 * sign
    row = lax.broadcasted_iota(jnp.int32, (plane, waves), 0)
    chosen = jnp.where(row == code, 1.0, 0.0).astype(BF)
    order = lax.broadcasted_iota(jnp.int32, (16, waves), 0)
    weight = jnp.where(order < 8, 1, jnp.where(height < 0, -1, 1)).astype(F32)
    picked = jnp.where(jnp.abs(height) == order % 8, weight, 0.0).astype(BF)
    count = dot_dims(picked, chosen, 1, 1)
    lane = lax.broadcasted_iota(jnp.int32, (16, plane), 1)
    k0 = (lane // columns).astype(F32)
    k1 = (lane % columns - reach).astype(F32)
    k2 = (lax.broadcasted_iota(jnp.int32, (16, plane), 0) % 8).astype(F32)
    strength = count / (1.0 + (k0 * k0 + k1 * k1 + k2 * k2) / 16.0)

    cosine, sine = plane_phases(position)
    cosine, sine = cosine.T, sine.T
    for m in range(orders):
        even = strength[m : m + 1]
        left_ref[m, :, :plane] = (cosine * even).astype(BF)
        left_ref[m, :, plane:] = (sine * even).astype(BF)
        if m:
            odd = strength[8 + m : 9 + m]
            left_ref[reach + m, :, :plane] = (sine * -odd).astype(BF)
            left_ref[reach + m, :, plane:] = (cosine * odd).astype(BF)
    zc, zs = turn_trig(position[2:3])
    zc_ref[...] = jnp.broadcast_to(zc, (rows, rows)).T
    zs_ref[...] = jnp.broadcast_to(zs, (rows, rows)).T


def prepare(wave_index, position, own, distances, w_rbf, w_filter):
    rows = position.shape[1]
    shapes = (
        jax.ShapeDtypeStruct((rows + extra_rows, own.shape[1]), BF),
        jax.ShapeDtypeStruct((2 * reach + 1, rows, 2 * plane), BF),
        jax.ShapeDtypeStruct((rows, rows), F32),
        jax.ShapeDtypeStruct((rows, rows), F32),
        jax.ShapeDtypeStruct(distances.shape, F32),
        jax.ShapeDtypeStruct((1,) + w_rbf.shape[1:], BF),
        jax.ShapeDtypeStruct((1,) + w_filter.shape[1:], BF),
    )
    inputs = (wave_index, position, own, distances, w_rbf, w_filter)
    return pl.pallas_call(
        prepare_kernel,
        out_shape=shapes,
        grid=(1,),
        in_specs=[whole(x) for x in inputs[:4]] + [whole(x) for x in shapes[-2:]],
        out_specs=(VM,) * len(shapes),
        compiler_params=limit,
        name="prepare",
    )(*[in_hbm(x) for x in inputs])


def coupling_kernel(places, rows, left_ref, zc_ref, zs_ref, *refs):
    count = max(p[0] for p in places) + 1
    packed, out_ref, right_ref, part_ref = refs[:count], refs[count], refs[count + 1], refs[count + 2]
    tile = 32
    for pair in range(0, len(places), 2):
        turn = pair // 2 % 2
        span = min(2, len(places) - pair)
        heights = []
        for side in range(span):
            which, start = places[pair + side]
            block = packed[which][start + rows : start + rows + extra_rows, :].astype(F32)
            position = (block[0:3, :rows] + block[0:3, rows : 2 * rows]) + block[3:6, :rows]
            cosine, sine = plane_phases(position)
            at = slice(side * rows, (side + 1) * rows)
            right_ref[turn, :plane, at] = cosine.astype(BF)
            right_ref[turn, plane:, at] = sine.astype(BF)
            heights.append(turn_trig(position[2:3]))
        wide = span * rows
        for m in range(2 * reach + 1):
            part_ref[turn, m, :, :wide] = dot(left_ref[m], right_ref[turn, :, :wide])
        for side in range(span):
            zc, zs = heights[side]
            at = slice(side * rows, (side + 1) * rows)
            for top in range(0, rows, tile):
                own = slice(top, top + tile)
                oc, os = zc_ref[own, :], zs_ref[own, :]
                c1 = oc * zc + os * zs
                s1 = os * zc - oc * zs
                twice = c1 + c1
                even, odd = part_ref[turn, reach, own, at], part_ref[turn, 2 * reach, own, at]
                even_last, odd_last = 0.0, 0.0
                for m in range(reach - 1, 0, -1):
                    even, even_last = part_ref[turn, m, own, at] + twice * even - even_last, even
                    odd, odd_last = part_ref[turn, reach + m, own, at] + twice * odd - odd_last, odd
                total = part_ref[turn, 0, own, at] + c1 * even - even_last + s1 * odd
                out_ref[own, pair * rows + side * rows : pair * rows + (side + 1) * rows] = total.astype(BF)


def coupling(prepared, arrays, places, rows):
    left, zc, zs = prepared
    return pl.pallas_call(
        functools.partial(coupling_kernel, tuple(places), rows),
        out_shape=jax.ShapeDtypeStruct((rows, len(places) * rows), BF),
        scratch_shapes=[
            pltpu.VMEM((2, 2 * plane, 2 * rows), BF),
            pltpu.VMEM((2, 2 * reach + 1, rows, 2 * rows), F32),
        ],
        in_specs=[pl.BlockSpec(memory_space=pltpu.VMEM)] * (3 + len(arrays)),
        out_specs=pl.BlockSpec(memory_space=pltpu.VMEM),
        name="coupling",
        compiler_params=limit,
    )(left, zc, zs, *arrays)


def coupling_of(prepared, arrays, places, blocks, rows):
    used = sorted({places[q][0] for q in blocks})
    spots = [(used.index(places[q][0]), places[q][1]) for q in blocks]
    return coupling(prepared, [arrays[n] for n in used], spots, rows)


def centers_of(count, rows):
    step = lax.broadcasted_iota(jnp.int32, (count, rows), 0).astype(F32)
    return 0.5 + 4.5 * step / (count - 1)


def filters_at(distance_ref, begin, count, centers, first, second):
    pieces = []
    for s in range(begin, begin + count):
        offset = distance_ref[s : s + 1, :] - centers
        pieces.append(jnp.exp(-4.0 * offset * offset).astype(BF))
    half = dot_dims(jnp.concatenate(pieces, axis=1), first, 0, 0)
    inner = (half + half * jnp.tanh(half)).astype(BF)
    return dot(inner, second).reshape(count, centers.shape[1], second.shape[1])


def filter_kernel(layer, distance_ref, rbf_ref, filter_ref, out_ref):
    group, rows, _ = out_ref.shape
    centers = centers_of(rbf_ref.shape[1], rows)
    first = rbf_ref[layer] * jnp.asarray(0.5, BF)
    for chunk in range(0, group, filter_group):
        made = filters_at(distance_ref, chunk, filter_group, centers, first, filter_ref[layer])
        out_ref[chunk : chunk + filter_group] = made.astype(BF)


def filters_of(distances, w_rbf, w_filter, layer, count):
    rows = distances.shape[1]
    width = w_filter.shape[2]
    return pl.pallas_call(
        functools.partial(filter_kernel, layer),
        out_shape=jax.ShapeDtypeStruct((count, rows, width), BF),
        in_specs=[VM] * 3,
        out_specs=VM,
        compiler_params=limit,
        name="filters",
    )(distances, w_rbf, w_filter)


def code_of(index):
    return jnp.where(index < 256, index, 255 - index).astype(F32).astype(BF)


def message_kernel(
    layer, index_ref, distance_ref, mask_ref, table_ref, rbf_ref, filter_ref, ready_ref, out_ref
):
    slots, rows = index_ref.shape
    reachable, width = table_ref.shape
    ready = ready_ref.shape[0]
    lane = code_of(lax.broadcasted_iota(jnp.int32, (rows, reachable), 1))
    centers = centers_of(rbf_ref.shape[1], rows)
    first = rbf_ref[layer] * jnp.asarray(0.5, BF)
    total = jnp.zeros((rows, width), F32)
    group = message_group
    starts = [n for pair in zip(range(0, ready, group), range(ready, slots, group)) for n in pair]
    starts += [n for n in range(0, slots, group) if n not in starts]
    for begin in starts:
        at = slice(begin, begin + group)
        code = code_of(index_ref[at, :]).astype(F32).T.astype(BF)
        cosine, _ = turn_trig(distance_ref[at, :] * 0.1)
        weight = (0.5 * (cosine + 1.0) * mask_ref[at, :].astype(F32)).T.astype(BF)
        picks = [
            jnp.where(lane == code[:, s : s + 1], weight[:, s : s + 1], jnp.zeros((), BF))
            for s in range(group)
        ]
        gathered = dot(jnp.concatenate(picks, axis=0), table_ref[...]).reshape(group, rows, width)
        if begin < ready:
            factors = ready_ref[at].astype(F32)
        else:
            factors = filters_at(distance_ref, begin, group, centers, first, filter_ref[layer])
        total = total + jnp.sum(gathered * factors, axis=0)
    out_ref[...] = total.astype(BF)


def messages(neighbours, distances, edge_mask, table, w_rbf, w_filter, layer, ready):
    inputs = (neighbours, distances, edge_mask, table, w_rbf, w_filter, ready)
    return pl.pallas_call(
        functools.partial(message_kernel, layer),
        out_shape=jax.ShapeDtypeStruct((neighbours.shape[1], table.shape[1]), BF),
        in_specs=[VM] * len(inputs),
        out_specs=VM,
        compiler_params=limit,
        name="messages",
    )(*inputs)


def gathered_field(places, rows, matrices, states):
    total = None
    for which, start, matrix, column in places:
        part = dot(
            matrices[matrix][:, column * rows : (column + 1) * rows], states[which][start : start + rows, :]
        )
        total = part if total is None else total + part
    return total


def partial_kernel(places, pairs, layer, message_ref, short_ref, *refs):
    matrices, states, total_ref, close_ref = refs[:pairs], refs[pairs:-2], refs[-2], refs[-1]
    total_ref[...] = gathered_field(places, message_ref.shape[0], matrices, states)
    close_ref[...] = dot(message_ref[...], short_ref[layer])


def partial_update(message, w_short, layer, matrices, arrays, places):
    shape = jax.ShapeDtypeStruct(message.shape, F32)
    return pl.pallas_call(
        functools.partial(partial_kernel, tuple(places), len(matrices), layer),
        out_shape=(shape, shape),
        in_specs=[VM] * (2 + len(matrices) + len(arrays)),
        out_specs=(VM, VM),
        compiler_params=limit,
        name="partial",
    )(message, w_short, *matrices, *arrays)


def update_kernel(places, pairs, begun, layer, before, after, own_ref, mixing_ref, long_ref, *refs):
    rows, _ = own_ref.shape
    head, matrices, states, out_ref = refs[:2], refs[2 : 2 + pairs], refs[2 + pairs : -1], refs[-1]
    total = gathered_field(places, rows, matrices, states)
    if begun:
        total = total + head[0][...]
        close = head[1][...]
    else:
        close = dot(head[0][...], head[1][layer])
    potential = dot((total * before).astype(BF), mixing_ref[layer]).astype(BF)
    field = (potential.astype(F32) * after).astype(BF)
    half = 0.5 * (close + dot(field, long_ref[layer]))
    out_ref[...] = (own_ref[...].astype(F32) + (half + half * jnp.tanh(half))).astype(BF)


def update(own, head, begun, mixing, long, layer, matrices, arrays, places, before, after):
    return pl.pallas_call(
        functools.partial(update_kernel, tuple(places), len(matrices), begun, layer, before, after),
        out_shape=jax.ShapeDtypeStruct(own.shape, BF),
        in_specs=[VM] * (5 + len(matrices) + len(arrays)),
        out_specs=VM,
        compiler_params=limit,
        name="update",
    )(own, mixing, long, *head, *matrices, *arrays)


def picked(spots, matrices, arrays):
    rows = sorted({spot[2] for spot in spots})
    used = sorted({spot[0] for spot in spots})
    spots = [(used.index(a), s, rows.index(m), c) for a, s, m, c in spots]
    return [matrices[m] for m in rows], [arrays[a] for a in used], spots


def swap(x, even, odd):
    count = lax.axis_size("atom")
    return lax.ppermute(x, "atom", [(i, i ^ (odd if i % 2 else even)) for i in range(count)])


def schedule(count, lean):
    bits = [1 << n for n in range(count.bit_length() - 1)][::-1]
    stages, have = [], [0]
    if len(bits) >= 4:
        far, near, side, last = bits[0], bits[1], bits[2], bits[-1]
        first = [far + near, far, near]
        early = first if lean else first + [side]
        sent = [0] + first if lean else first
        second = [side + q for q in sent]
        stages.append([(mask, mask, [0], [mask]) for mask in early + [last]])
        stages.append([(side, side, sent, second), (last, last, early, [last + q for q in early])])
        stages.append([(last, last, second, [last + q for q in second])])
        have = [0] + [q for stage in stages for item in stage for q in item[3]]
        bits = bits[3:-1]
    for bit in bits:
        stages.append([(bit, bit, list(have), [q ^ bit for q in have])])
        have = have + [q ^ bit for q in have]
    return stages


def exchange(arrays, places, stage, size):
    arrays, places = list(arrays), dict(places)
    sends = []
    for _, _, wanted, _ in stage:
        parts = [
            lax.slice_in_dim(arrays[places[q][0]], places[q][1], places[q][1] + size, axis=0)
            for q in wanted
        ]
        sends.append(parts[0] if len(parts) == 1 else jnp.concatenate(parts, axis=0))
    for (even, odd, _, labels), sent in zip(stage, sends):
        arrays.append(swap(sent, even, odd))
        for n, q in enumerate(labels):
            places[q] = (len(arrays) - 1, n * size)
    return arrays, places


def neighbour_table(own, close, even):
    count = lax.axis_size("atom")
    far = lax.ppermute(
        own, "atom", [(i, (i + (count - 1 if i % 2 == 0 else 1)) % count) for i in range(count)]
    )
    return jnp.concatenate([jnp.where(even, far, close), own, jnp.where(even, close, far)], axis=0)


def per_device(
    features,
    fractional,
    distances,
    neighbours,
    edge_mask,
    wave_index,
    w_rbf,
    w_filter,
    w_mixing,
    w_short,
    w_long,
):
    rows, _ = features.shape
    slots = neighbours.shape[0]
    bricks = lax.axis_size("atom")
    before = 1.0 / math.sqrt(rows * bricks)
    after = 4.0 / math.sqrt(wave_index.shape[1])
    even = lax.axis_index("atom") % 2 == 0

    packed, *prepared, near_distances, first_rbf, first_filter = prepare(
        wave_index, fractional, features, distances, w_rbf, w_filter
    )
    state = features
    matrices, where = [], {}

    def couple(arrays, places):
        ready = [q for q in places if q not in where]
        if len(places) < bricks:
            ready = ready[: len(ready) // 2 * 2]
        matrix = coupling_of(prepared, arrays, places, ready, rows)
        where.update({q: (len(matrices), n) for n, q in enumerate(ready)})
        matrices.append(matrix)

    for layer in range(w_rbf.shape[0]):
        block = state if layer else packed
        stages = schedule(bricks, False)
        size = block.shape[0]
        arrays, places = exchange([block], {0: (0, 0)}, stages[0], size)
        close = arrays[places[1][0]][:rows] if 1 in places else swap(state, 1, 1)
        table = neighbour_table(state, close, even)
        if layer:
            edge = (distances, w_rbf, w_filter, layer)
        else:
            edge = (near_distances, first_rbf, first_filter, 0)
        ready = filters_of(*edge, slots // 2)
        message = messages(neighbours, edge[0], edge_mask, table, *edge[1:], ready)
        for stage in stages[1:]:
            if layer == 0:
                couple(arrays, places)
            early = list(places)
            arrays, places = exchange(arrays, places, stage, size)
        if layer == 0:
            couple(arrays, places)
            early = []
        spot = {q: places[q] + where[q] for q in places}
        head, late = (message, w_short), [q for q in places if q not in early]
        if early:
            used, held, spots = picked([spot[q] for q in early], matrices, arrays)
            head = partial_update(message, w_short, layer, used, held, spots)
        used, held, spots = picked([spot[q] for q in late], matrices, arrays)
        state = update(
            state, head, bool(early), w_mixing, w_long, layer, used, held, spots, before, after
        )
    return state


def solution(mesh):
    along = P(None, ("rep", "atom"))
    in_specs = (P(("rep", "atom"), None), along, along, along, along) + (P(),) * 6
    return jax.shard_map(
        per_device, mesh=mesh, in_specs=in_specs, out_specs=P(("rep", "atom"), None), check_vma=False
    )
```

```python
import functools
import math

import jax
import jax.numpy as jnp
from jax import lax
from jax.experimental import pallas as pl
from jax.experimental.pallas import tpu as pltpu
from jax.sharding import PartitionSpec as P


message_group = 16
filter_group = 8
reach = 6
orders = reach + 1
columns = 16
plane = (reach + 2) * columns
extra_rows = 16
limit = pltpu.CompilerParams(vmem_limit_bytes=20 << 20)
BF = jnp.bfloat16
F32 = jnp.float32


def dot(a, b):
    return jnp.dot(a, b, preferred_element_type=F32)


def dot_dims(a, b, ca, cb):
    return lax.dot_general(a, b, (((ca,), (cb,)), ((), ())), preferred_element_type=F32)


def turn_trig(turns):
    part = turns - jnp.round(turns)
    angle = part * (2.0 * math.pi)
    square = angle * angle
    cosine = jnp.full_like(square, 1.0 / math.factorial(18))
    for n in range(16, -2, -2):
        cosine = cosine * -square + 1.0 / math.factorial(n)
    sine = jnp.full_like(square, 1.0 / math.factorial(19))
    for n in range(17, -1, -2):
        sine = sine * -square + 1.0 / math.factorial(n)
    return cosine, sine * angle


def plane_phases(position):
    rows = position.shape[1]
    x, y = position[0:1], position[1:2]
    first = lax.broadcasted_iota(jnp.int32, (8, rows), 0).astype(F32)
    second = lax.broadcasted_iota(jnp.int32, (columns, rows), 0).astype(F32) - reach
    xc, xs = turn_trig(first * x)
    yc, ys = turn_trig(second * y)
    cosines, sines = [], []
    for a in range(plane // columns):
        pc, ps = xc[a : a + 1], xs[a : a + 1]
        cosines.append(pc * yc - ps * ys)
        sines.append(pc * ys + ps * yc)
    return jnp.concatenate(cosines, axis=0), jnp.concatenate(sines, axis=0)


def in_hbm(x):
    return pltpu.with_memory_space_constraint(x, pltpu.HBM)


VM = pl.BlockSpec(memory_space=pltpu.VMEM)
RAW = pl.BlockSpec(memory_space=pl.ANY)


def whole(x):
    return pl.BlockSpec(x.shape, lambda i: (0,) * len(x.shape))


def prepare_kernel(
    wave_ref, position_ref, own_ref, distance_ref, rbf_ref, filter_ref,
    packed_ref, left_ref, zc_ref, zs_ref, distance_out, rbf_out, filter_out,
):
    distance_out[...] = distance_ref[...]
    rbf_out[...] = rbf_ref[...]
    filter_out[...] = filter_ref[...]
    rows = position_ref.shape[1]
    position = position_ref[...]
    top = position.astype(BF)
    rest = position - top.astype(F32)
    middle = rest.astype(BF)
    low = (rest - middle.astype(F32)).astype(BF)
    blank = jnp.zeros((extra_rows, 2 * rows), BF)
    packed_ref[:rows, :] = own_ref[...]
    packed_ref[rows:, :] = blank
    packed_ref[rows : rows + 3, :rows] = top
    packed_ref[rows : rows + 3, rows : 2 * rows] = middle
    packed_ref[rows + 3 : rows + 6, :rows] = low

    waves = wave_ref.shape[1]
    m0, m1, m2 = wave_ref[0:1, :], wave_ref[1:2, :], wave_ref[2:3, :]
    flip = jnp.logical_or(m0 < 0, jnp.logical_and(m0 == 0, m1 < 0))
    sign = jnp.where(flip, -1, 1)
    code = m0 * sign * columns + m1 * sign + reach
    height = m2 * sign
    row = lax.broadcasted_iota(jnp.int32, (plane, waves), 0)
    chosen = jnp.where(row == code, 1.0, 0.0).astype(BF)
    order = lax.broadcasted_iota(jnp.int32, (16, waves), 0)
    weight = jnp.where(order < 8, 1, jnp.where(height < 0, -1, 1)).astype(F32)
    picked = jnp.where(jnp.abs(height) == order % 8, weight, 0.0).astype(BF)
    count = dot_dims(picked, chosen, 1, 1)
    lane = lax.broadcasted_iota(jnp.int32, (16, plane), 1)
    k0 = (lane // columns).astype(F32)
    k1 = (lane % columns - reach).astype(F32)
    k2 = (lax.broadcasted_iota(jnp.int32, (16, plane), 0) % 8).astype(F32)
    strength = count / (1.0 + (k0 * k0 + k1 * k1 + k2 * k2) / 16.0)

    cosine, sine = plane_phases(position)
    cosine, sine = cosine.T, sine.T
    for m in range(orders):
        even = strength[m : m + 1]
        left_ref[m, :, :plane] = (cosine * even).astype(BF)
        left_ref[m, :, plane:] = (sine * even).astype(BF)
        if m:
            odd = strength[8 + m : 9 + m]
            left_ref[reach + m, :, :plane] = (sine * -odd).astype(BF)
            left_ref[reach + m, :, plane:] = (cosine * odd).astype(BF)
    zc, zs = turn_trig(position[2:3])
    zc_ref[...] = jnp.broadcast_to(zc, (rows, rows)).T
    zs_ref[...] = jnp.broadcast_to(zs, (rows, rows)).T


def prepare(wave_index, position, own, distances, w_rbf, w_filter):
    rows = position.shape[1]
    shapes = (
        jax.ShapeDtypeStruct((rows + extra_rows, own.shape[1]), BF),
        jax.ShapeDtypeStruct((2 * reach + 1, rows, 2 * plane), BF),
        jax.ShapeDtypeStruct((rows, rows), F32),
        jax.ShapeDtypeStruct((rows, rows), F32),
        jax.ShapeDtypeStruct(distances.shape, F32),
        jax.ShapeDtypeStruct((1,) + w_rbf.shape[1:], BF),
        jax.ShapeDtypeStruct((1,) + w_filter.shape[1:], BF),
    )
    inputs = (wave_index, position, own, distances, w_rbf, w_filter)
    return pl.pallas_call(
        prepare_kernel,
        out_shape=shapes,
        grid=(1,),
        in_specs=[whole(x) for x in inputs[:4]] + [whole(x) for x in shapes[-2:]],
        out_specs=(VM,) * len(shapes),
        compiler_params=limit,
        name="prepare",
    )(*[in_hbm(x) for x in inputs])


def coupling_kernel(places, rows, left_ref, zc_ref, zs_ref, *refs):
    count = max(p[0] for p in places) + 1
    packed, out_ref, right_ref, part_ref = refs[:count], refs[count], refs[count + 1], refs[count + 2]
    tile = 64
    for pair in range(0, len(places), 2):
        turn = pair // 2 % 2
        span = min(2, len(places) - pair)
        heights = []
        for side in range(span):
            which, start = places[pair + side]
            block = packed[which][start + rows : start + rows + extra_rows, :].astype(F32)
            position = (block[0:3, :rows] + block[0:3, rows : 2 * rows]) + block[3:6, :rows]
            cosine, sine = plane_phases(position)
            at = slice(side * rows, (side + 1) * rows)
            right_ref[turn, :plane, at] = cosine.astype(BF)
            right_ref[turn, plane:, at] = sine.astype(BF)
            heights.append(turn_trig(position[2:3]))
        wide = span * rows
        for m in range(2 * reach + 1):
            part_ref[turn, m, :, :wide] = dot(left_ref[m], right_ref[turn, :, :wide])
        for side in range(span):
            zc, zs = heights[side]
            at = slice(side * rows, (side + 1) * rows)
            for top in range(0, rows, tile):
                own = slice(top, top + tile)
                oc, os = zc_ref[own, :], zs_ref[own, :]
                c1 = oc * zc + os * zs
                s1 = os * zc - oc * zs
                twice = c1 + c1
                even, odd = part_ref[turn, reach, own, at], part_ref[turn, 2 * reach, own, at]
                even_last, odd_last = 0.0, 0.0
                for m in range(reach - 1, 0, -1):
                    even, even_last = part_ref[turn, m, own, at] + twice * even - even_last, even
                    odd, odd_last = part_ref[turn, reach + m, own, at] + twice * odd - odd_last, odd
                total = part_ref[turn, 0, own, at] + c1 * even - even_last + s1 * odd
                out_ref[own, pair * rows + side * rows : pair * rows + (side + 1) * rows] = total.astype(BF)


def coupling(prepared, arrays, places, rows):
    left, zc, zs = prepared
    return pl.pallas_call(
        functools.partial(coupling_kernel, tuple(places), rows),
        out_shape=jax.ShapeDtypeStruct((rows, len(places) * rows), BF),
        scratch_shapes=[
            pltpu.VMEM((2, 2 * plane, 2 * rows), BF),
            pltpu.VMEM((2, 2 * reach + 1, rows, 2 * rows), F32),
        ],
        in_specs=[pl.BlockSpec(memory_space=pltpu.VMEM)] * (3 + len(arrays)),
        out_specs=pl.BlockSpec(memory_space=pltpu.VMEM),
        name="coupling",
        compiler_params=limit,
    )(left, zc, zs, *arrays)


def coupling_of(prepared, arrays, places, blocks, rows):
    used = sorted({places[q][0] for q in blocks})
    spots = [(used.index(places[q][0]), places[q][1]) for q in blocks]
    return coupling(prepared, [arrays[n] for n in used], spots, rows)


def centers_of(count, rows):
    step = lax.broadcasted_iota(jnp.int32, (count, rows), 0).astype(F32)
    return 0.5 + 4.5 * step / (count - 1)


def filters_at(distance_ref, begin, count, centers, first, second):
    pieces = []
    for s in range(begin, begin + count):
        offset = distance_ref[s : s + 1, :] - centers
        pieces.append(jnp.exp(-4.0 * offset * offset).astype(BF))
    half = dot_dims(jnp.concatenate(pieces, axis=1), first, 0, 0)
    inner = (half + half * jnp.tanh(half)).astype(BF)
    return dot(inner, second).reshape(count, centers.shape[1], second.shape[1])


def filter_kernel(layer, distance_ref, rbf_ref, filter_ref, out_ref):
    group, rows, _ = out_ref.shape
    centers = centers_of(rbf_ref.shape[1], rows)
    first = rbf_ref[layer] * jnp.asarray(0.5, BF)
    for chunk in range(0, group, filter_group):
        made = filters_at(distance_ref, chunk, filter_group, centers, first, filter_ref[layer])
        out_ref[chunk : chunk + filter_group] = made.astype(BF)


def filters_of(distances, w_rbf, w_filter, layer, count):
    rows = distances.shape[1]
    width = w_filter.shape[2]
    return pl.pallas_call(
        functools.partial(filter_kernel, layer),
        out_shape=jax.ShapeDtypeStruct((count, rows, width), BF),
        in_specs=[VM] * 3,
        out_specs=VM,
        compiler_params=limit,
        name="filters",
    )(distances, w_rbf, w_filter)


def code_of(index):
    return jnp.where(index < 256, index, 255 - index).astype(F32).astype(BF)


def message_kernel(
    layer, index_ref, distance_ref, mask_ref, table_ref, rbf_ref, filter_ref, ready_ref, out_ref
):
    slots, rows = index_ref.shape
    reachable, width = table_ref.shape
    ready = ready_ref.shape[0]
    lane = code_of(lax.broadcasted_iota(jnp.int32, (rows, reachable), 1))
    centers = centers_of(rbf_ref.shape[1], rows)
    first = rbf_ref[layer] * jnp.asarray(0.5, BF)
    total = jnp.zeros((rows, width), F32)
    group = message_group
    starts = [n for pair in zip(range(0, ready, group), range(ready, slots, group)) for n in pair]
    starts += [n for n in range(0, slots, group) if n not in starts]
    for begin in starts:
        at = slice(begin, begin + group)
        code = code_of(index_ref[at, :]).astype(F32).T.astype(BF)
        cosine, _ = turn_trig(distance_ref[at, :] * 0.1)
        weight = (0.5 * (cosine + 1.0) * mask_ref[at, :].astype(F32)).T.astype(BF)
        picks = [
            jnp.where(lane == code[:, s : s + 1], weight[:, s : s + 1], jnp.zeros((), BF))
            for s in range(group)
        ]
        gathered = dot(jnp.concatenate(picks, axis=0), table_ref[...]).reshape(group, rows, width)
        if begin < ready:
            factors = ready_ref[at].astype(F32)
        else:
            factors = filters_at(distance_ref, begin, group, centers, first, filter_ref[layer])
        total = total + jnp.sum(gathered * factors, axis=0)
    out_ref[...] = total.astype(BF)


def messages(neighbours, distances, edge_mask, table, w_rbf, w_filter, layer, ready):
    inputs = (neighbours, distances, edge_mask, table, w_rbf, w_filter, ready)
    return pl.pallas_call(
        functools.partial(message_kernel, layer),
        out_shape=jax.ShapeDtypeStruct((neighbours.shape[1], table.shape[1]), BF),
        in_specs=[VM] * len(inputs),
        out_specs=VM,
        compiler_params=limit,
        name="messages",
    )(*inputs)


def gathered_field(places, rows, matrices, states):
    total = None
    for which, start, matrix, column in places:
        part = dot(
            matrices[matrix][:, column * rows : (column + 1) * rows], states[which][start : start + rows, :]
        )
        total = part if total is None else total + part
    return total


def partial_kernel(places, pairs, layer, message_ref, short_ref, mixing_ref, long_ref, *refs):
    matrices, states = refs[:pairs], refs[pairs:-3]
    total_ref, close_ref, joint_ref = refs[-3:]
    total_ref[...] = gathered_field(places, message_ref.shape[0], matrices, states)
    close_ref[...] = dot(message_ref[...], short_ref[layer])
    joint_ref[...] = dot(mixing_ref[layer], long_ref[layer]).astype(BF)


def partial_update(message, w_short, w_mixing, w_long, layer, matrices, arrays, places):
    shape = jax.ShapeDtypeStruct(message.shape, F32)
    return pl.pallas_call(
        functools.partial(partial_kernel, tuple(places), len(matrices), layer),
        out_shape=(shape, shape, jax.ShapeDtypeStruct(w_mixing.shape[1:], BF)),
        in_specs=[VM] * (4 + len(matrices) + len(arrays)),
        out_specs=(VM,) * 3,
        compiler_params=limit,
        name="partial",
    )(message, w_short, w_mixing, w_long, *matrices, *arrays)


def update_kernel(places, pairs, scale, own_ref, total_ref, close_ref, joint_ref, *refs):
    matrices, states, out_ref = refs[:pairs], refs[pairs:-1], refs[-1]
    total = total_ref[...] + gathered_field(places, own_ref.shape[0], matrices, states)
    half = 0.5 * (close_ref[...] + dot((total * scale).astype(BF), joint_ref[...]))
    out_ref[...] = (own_ref[...].astype(F32) + (half + half * jnp.tanh(half))).astype(BF)


def update(own, head, matrices, arrays, places, scale):
    return pl.pallas_call(
        functools.partial(update_kernel, tuple(places), len(matrices), scale),
        out_shape=jax.ShapeDtypeStruct(own.shape, BF),
        in_specs=[VM] * (4 + len(matrices) + len(arrays)),
        out_specs=VM,
        compiler_params=limit,
        name="update",
    )(own, *head, *matrices, *arrays)


def picked(spots, matrices, arrays):
    rows = sorted({spot[2] for spot in spots})
    used = sorted({spot[0] for spot in spots})
    spots = [(used.index(a), s, rows.index(m), c) for a, s, m, c in spots]
    return [matrices[m] for m in rows], [arrays[a] for a in used], spots


def swap(x, even, odd):
    count = lax.axis_size("atom")
    return lax.ppermute(x, "atom", [(i, i ^ (odd if i % 2 else even)) for i in range(count)])


def schedule(count, lean):
    bits = [1 << n for n in range(count.bit_length() - 1)][::-1]
    stages, have = [], [0]
    if len(bits) >= 4:
        far, near, side, last = bits[0], bits[1], bits[2], bits[-1]
        first = [far + near, far, near]
        early = first if lean else first + [side]
        sent = [0] + first if lean else first
        second = [side + q for q in sent]
        stages.append([(mask, mask, [0], [mask]) for mask in early + [last]])
        stages.append([(side, side, sent, second), (last, last, early, [last + q for q in early])])
        stages.append([(last, last, second, [last + q for q in second])])
        have = [0] + [q for stage in stages for item in stage for q in item[3]]
        bits = bits[3:-1]
    for bit in bits:
        stages.append([(bit, bit, list(have), [q ^ bit for q in have])])
        have = have + [q ^ bit for q in have]
    return stages


def exchange(arrays, places, stage, size):
    arrays, places = list(arrays), dict(places)
    sends = []
    for _, _, wanted, _ in stage:
        parts = [
            lax.slice_in_dim(arrays[places[q][0]], places[q][1], places[q][1] + size, axis=0)
            for q in wanted
        ]
        sends.append(parts[0] if len(parts) == 1 else jnp.concatenate(parts, axis=0))
    for (even, odd, _, labels), sent in zip(stage, sends):
        arrays.append(swap(sent, even, odd))
        for n, q in enumerate(labels):
            places[q] = (len(arrays) - 1, n * size)
    return arrays, places


def neighbour_table(own, close, even):
    count = lax.axis_size("atom")
    far = lax.ppermute(
        own, "atom", [(i, (i + (count - 1 if i % 2 == 0 else 1)) % count) for i in range(count)]
    )
    return jnp.concatenate([jnp.where(even, far, close), own, jnp.where(even, close, far)], axis=0)


def per_device(
    features,
    fractional,
    distances,
    neighbours,
    edge_mask,
    wave_index,
    w_rbf,
    w_filter,
    w_mixing,
    w_short,
    w_long,
):
    rows, _ = features.shape
    slots = neighbours.shape[0]
    bricks = lax.axis_size("atom")
    before = 1.0 / math.sqrt(rows * bricks)
    after = 4.0 / math.sqrt(wave_index.shape[1])
    even = lax.axis_index("atom") % 2 == 0

    packed, *prepared, near_distances, first_rbf, first_filter = prepare(
        wave_index, fractional, features, distances, w_rbf, w_filter
    )
    state = features
    matrices, where = [], {}

    def couple(arrays, places):
        ready = [q for q in places if q not in where]
        if len(places) < bricks:
            ready = ready[: len(ready) // 2 * 2]
        matrix = coupling_of(prepared, arrays, places, ready, rows)
        where.update({q: (len(matrices), n) for n, q in enumerate(ready)})
        matrices.append(matrix)

    for layer in range(w_rbf.shape[0]):
        block = state if layer else packed
        stages = schedule(bricks, False)
        size = block.shape[0]
        arrays, places = exchange([block], {0: (0, 0)}, stages[0], size)
        close = arrays[places[1][0]][:rows] if 1 in places else swap(state, 1, 1)
        table = neighbour_table(state, close, even)
        if layer:
            edge = (distances, w_rbf, w_filter, layer)
        else:
            edge = (near_distances, first_rbf, first_filter, 0)
        ready = filters_of(*edge, slots // 2)
        message = messages(neighbours, edge[0], edge_mask, table, *edge[1:], ready)
        for stage in stages[1:]:
            if layer == 0:
                couple(arrays, places)
            early = list(places)
            arrays, places = exchange(arrays, places, stage, size)
        early = [q for q in early if layer or q in where]
        spot = {q: places[q] + where[q] for q in early}
        used, held, spots = picked([spot[q] for q in early], matrices, arrays)
        head = partial_update(message, w_short, w_mixing, w_long, layer, used, held, spots)
        if layer == 0:
            couple(arrays, places)
        spot = {q: places[q] + where[q] for q in places if q not in early}
        used, held, spots = picked(list(spot.values()), matrices, arrays)
        state = update(state, head, used, held, spots, before * after)
    return state


def solution(mesh):
    along = P(None, ("rep", "atom"))
    in_specs = (P(("rep", "atom"), None), along, along, along, along) + (P(),) * 6
    return jax.shard_map(
        per_device, mesh=mesh, in_specs=in_specs, out_specs=P(("rep", "atom"), None), check_vma=False
    )
```

```python
import functools
import math

import jax
import jax.numpy as jnp
from jax import lax
from jax.experimental import pallas as pl
from jax.experimental.pallas import tpu as pltpu
from jax.sharding import PartitionSpec as P


message_group = 16
filter_group = 8
reach = 6
orders = reach + 1
columns = 16
plane = (reach + 2) * columns
extra_rows = 16
limit = pltpu.CompilerParams(vmem_limit_bytes=20 << 20)
BF = jnp.bfloat16
F32 = jnp.float32


def dot(a, b):
    return jnp.dot(a, b, preferred_element_type=F32)


def dot_dims(a, b, ca, cb):
    return lax.dot_general(a, b, (((ca,), (cb,)), ((), ())), preferred_element_type=F32)


def turn_trig(turns):
    part = turns - jnp.round(turns)
    angle = part * (2.0 * math.pi)
    square = angle * angle
    cosine = jnp.full_like(square, 1.0 / math.factorial(18))
    for n in range(16, -2, -2):
        cosine = cosine * -square + 1.0 / math.factorial(n)
    sine = jnp.full_like(square, 1.0 / math.factorial(19))
    for n in range(17, -1, -2):
        sine = sine * -square + 1.0 / math.factorial(n)
    return cosine, sine * angle


def plane_phases(position):
    rows = position.shape[1]
    x, y = position[0:1], position[1:2]
    first = lax.broadcasted_iota(jnp.int32, (8, rows), 0).astype(F32)
    second = lax.broadcasted_iota(jnp.int32, (columns, rows), 0).astype(F32) - reach
    xc, xs = turn_trig(jnp.where(first > reach, position[2:3], first * x))
    yc, ys = turn_trig(second * y)
    cosines, sines = [], []
    for a in range(plane // columns):
        pc, ps = xc[a : a + 1], xs[a : a + 1]
        cosines.append(pc * yc - ps * ys)
        sines.append(pc * ys + ps * yc)
    height = xc[orders : orders + 1], xs[orders : orders + 1]
    return jnp.concatenate(cosines, axis=0), jnp.concatenate(sines, axis=0), height


def in_hbm(x):
    return pltpu.with_memory_space_constraint(x, pltpu.HBM)


VM = pl.BlockSpec(memory_space=pltpu.VMEM)
RAW = pl.BlockSpec(memory_space=pl.ANY)


def whole(x):
    return pl.BlockSpec(x.shape, lambda i: (0,) * len(x.shape))


def prepare_kernel(
    wave_ref, position_ref, own_ref, distance_ref, rbf_ref, filter_ref,
    packed_ref, left_ref, zc_ref, zs_ref, distance_out, rbf_out, filter_out,
):
    distance_out[...] = distance_ref[...]
    rbf_out[...] = rbf_ref[...]
    filter_out[...] = filter_ref[...]
    rows = position_ref.shape[1]
    position = position_ref[...]
    top = position.astype(BF)
    rest = position - top.astype(F32)
    middle = rest.astype(BF)
    low = (rest - middle.astype(F32)).astype(BF)
    blank = jnp.zeros((extra_rows, 2 * rows), BF)
    packed_ref[:rows, :] = own_ref[...]
    packed_ref[rows:, :] = blank
    packed_ref[rows : rows + 3, :rows] = top
    packed_ref[rows : rows + 3, rows : 2 * rows] = middle
    packed_ref[rows + 3 : rows + 6, :rows] = low

    waves = wave_ref.shape[1]
    m0, m1, m2 = wave_ref[0:1, :], wave_ref[1:2, :], wave_ref[2:3, :]
    flip = jnp.logical_or(m0 < 0, jnp.logical_and(m0 == 0, m1 < 0))
    sign = jnp.where(flip, -1, 1)
    code = m0 * sign * columns + m1 * sign + reach
    height = m2 * sign
    row = lax.broadcasted_iota(jnp.int32, (plane, waves), 0)
    chosen = jnp.where(row == code, 1.0, 0.0).astype(BF)
    order = lax.broadcasted_iota(jnp.int32, (16, waves), 0)
    weight = jnp.where(order < 8, 1, jnp.where(height < 0, -1, 1)).astype(F32)
    picked = jnp.where(jnp.abs(height) == order % 8, weight, 0.0).astype(BF)
    count = dot_dims(picked, chosen, 1, 1)
    lane = lax.broadcasted_iota(jnp.int32, (16, plane), 1)
    k0 = (lane // columns).astype(F32)
    k1 = (lane % columns - reach).astype(F32)
    k2 = (lax.broadcasted_iota(jnp.int32, (16, plane), 0) % 8).astype(F32)
    strength = count / (1.0 + (k0 * k0 + k1 * k1 + k2 * k2) / 16.0)

    cosine, sine, (zc, zs) = plane_phases(position)
    cosine, sine = cosine.T, sine.T
    for m in range(orders):
        even = strength[m : m + 1]
        left_ref[m, :, :plane] = (cosine * even).astype(BF)
        left_ref[m, :, plane:] = (sine * even).astype(BF)
        if m:
            odd = strength[8 + m : 9 + m]
            left_ref[reach + m, :, :plane] = (sine * -odd).astype(BF)
            left_ref[reach + m, :, plane:] = (cosine * odd).astype(BF)
    zc_ref[...] = jnp.broadcast_to(zc, (rows, rows)).T
    zs_ref[...] = jnp.broadcast_to(zs, (rows, rows)).T


def prepare(wave_index, position, own, distances, w_rbf, w_filter):
    rows = position.shape[1]
    shapes = (
        jax.ShapeDtypeStruct((rows + extra_rows, own.shape[1]), BF),
        jax.ShapeDtypeStruct((2 * reach + 1, rows, 2 * plane), BF),
        jax.ShapeDtypeStruct((rows, rows), F32),
        jax.ShapeDtypeStruct((rows, rows), F32),
        jax.ShapeDtypeStruct(distances.shape, F32),
        jax.ShapeDtypeStruct((1,) + w_rbf.shape[1:], BF),
        jax.ShapeDtypeStruct((1,) + w_filter.shape[1:], BF),
    )
    inputs = (wave_index, position, own, distances, w_rbf, w_filter)
    return pl.pallas_call(
        prepare_kernel,
        out_shape=shapes,
        grid=(1,),
        in_specs=[whole(x) for x in inputs[:4]] + [whole(x) for x in shapes[-2:]],
        out_specs=(VM,) * len(shapes),
        compiler_params=limit,
        name="prepare",
    )(*[in_hbm(x) for x in inputs])


def coupling_kernel(places, rows, left_ref, zc_ref, zs_ref, *refs):
    count = max(p[0] for p in places) + 1
    packed, out_ref, right_ref, part_ref = refs[:count], refs[count], refs[count + 1], refs[count + 2]
    tile = 64
    for pair in range(0, len(places), 2):
        turn = pair // 2 % 2
        span = min(2, len(places) - pair)
        heights = []
        for side in range(span):
            which, start = places[pair + side]
            block = packed[which][start + rows : start + rows + extra_rows, :].astype(F32)
            position = (block[0:3, :rows] + block[0:3, rows : 2 * rows]) + block[3:6, :rows]
            cosine, sine, height = plane_phases(position)
            at = slice(side * rows, (side + 1) * rows)
            right_ref[turn, :plane, at] = cosine.astype(BF)
            right_ref[turn, plane:, at] = sine.astype(BF)
            heights.append(height)
        wide = span * rows
        for m in range(2 * reach + 1):
            part_ref[turn, m, :, :wide] = dot(left_ref[m], right_ref[turn, :, :wide])
        for side in range(span):
            zc, zs = heights[side]
            at = slice(side * rows, (side + 1) * rows)
            for top in range(0, rows, tile):
                own = slice(top, top + tile)
                oc, os = zc_ref[own, :], zs_ref[own, :]
                c1 = oc * zc + os * zs
                s1 = os * zc - oc * zs
                twice = c1 + c1
                even, odd = part_ref[turn, reach, own, at], part_ref[turn, 2 * reach, own, at]
                even_last, odd_last = 0.0, 0.0
                for m in range(reach - 1, 0, -1):
                    even, even_last = part_ref[turn, m, own, at] + twice * even - even_last, even
                    odd, odd_last = part_ref[turn, reach + m, own, at] + twice * odd - odd_last, odd
                total = part_ref[turn, 0, own, at] + c1 * even - even_last + s1 * odd
                out_ref[own, pair * rows + side * rows : pair * rows + (side + 1) * rows] = total.astype(BF)


def coupling(prepared, arrays, places, rows):
    left, zc, zs = prepared
    return pl.pallas_call(
        functools.partial(coupling_kernel, tuple(places), rows),
        out_shape=jax.ShapeDtypeStruct((rows, len(places) * rows), BF),
        scratch_shapes=[
            pltpu.VMEM((2, 2 * plane, 2 * rows), BF),
            pltpu.VMEM((2, 2 * reach + 1, rows, 2 * rows), F32),
        ],
        in_specs=[pl.BlockSpec(memory_space=pltpu.VMEM)] * (3 + len(arrays)),
        out_specs=pl.BlockSpec(memory_space=pltpu.VMEM),
        name="coupling",
        compiler_params=limit,
    )(left, zc, zs, *arrays)


def coupling_of(prepared, arrays, places, blocks, rows):
    used = sorted({places[q][0] for q in blocks})
    spots = [(used.index(places[q][0]), places[q][1]) for q in blocks]
    return coupling(prepared, [arrays[n] for n in used], spots, rows)


def centers_of(count, rows):
    step = lax.broadcasted_iota(jnp.int32, (count, rows), 0).astype(F32)
    return 0.5 + 4.5 * step / (count - 1)


def filters_at(distance_ref, begin, count, centers, first, second):
    pieces = []
    for s in range(begin, begin + count):
        offset = distance_ref[s : s + 1, :] - centers
        pieces.append(jnp.exp(-4.0 * offset * offset).astype(BF))
    half = dot_dims(jnp.concatenate(pieces, axis=1), first, 0, 0)
    inner = (half + half * jnp.tanh(half)).astype(BF)
    return dot(inner, second).reshape(count, centers.shape[1], second.shape[1])


def filter_kernel(layer, distance_ref, rbf_ref, filter_ref, out_ref):
    group, rows, _ = out_ref.shape
    centers = centers_of(rbf_ref.shape[1], rows)
    first = rbf_ref[layer] * jnp.asarray(0.5, BF)
    for chunk in range(0, group, filter_group):
        made = filters_at(distance_ref, chunk, filter_group, centers, first, filter_ref[layer])
        out_ref[chunk : chunk + filter_group] = made.astype(BF)


def filters_of(distances, w_rbf, w_filter, layer, count):
    rows = distances.shape[1]
    width = w_filter.shape[2]
    return pl.pallas_call(
        functools.partial(filter_kernel, layer),
        out_shape=jax.ShapeDtypeStruct((count, rows, width), BF),
        in_specs=[VM] * 3,
        out_specs=VM,
        compiler_params=limit,
        name="filters",
    )(distances, w_rbf, w_filter)


def code_of(index):
    return jnp.where(index < 256, index, 255 - index).astype(F32).astype(BF)


def message_kernel(
    layer, index_ref, distance_ref, mask_ref, table_ref, rbf_ref, filter_ref, ready_ref, out_ref
):
    slots, rows = index_ref.shape
    reachable, width = table_ref.shape
    ready = ready_ref.shape[0]
    lane = code_of(lax.broadcasted_iota(jnp.int32, (rows, reachable), 1))
    centers = centers_of(rbf_ref.shape[1], rows)
    first = rbf_ref[layer] * jnp.asarray(0.5, BF)
    total = jnp.zeros((rows, width), F32)
    group = message_group
    starts = [n for pair in zip(range(0, ready, group), range(ready, slots, group)) for n in pair]
    starts += [n for n in range(0, slots, group) if n not in starts]
    for begin in starts:
        at = slice(begin, begin + group)
        code = code_of(index_ref[at, :]).astype(F32).T.astype(BF)
        cosine, _ = turn_trig(distance_ref[at, :] * 0.1)
        weight = (0.5 * (cosine + 1.0) * mask_ref[at, :].astype(F32)).T.astype(BF)
        picks = [
            jnp.where(lane == code[:, s : s + 1], weight[:, s : s + 1], jnp.zeros((), BF))
            for s in range(group)
        ]
        gathered = dot(jnp.concatenate(picks, axis=0), table_ref[...]).reshape(group, rows, width)
        if begin < ready:
            factors = ready_ref[at].astype(F32)
        else:
            factors = filters_at(distance_ref, begin, group, centers, first, filter_ref[layer])
        total = total + jnp.sum(gathered * factors, axis=0)
    out_ref[...] = total.astype(BF)


def messages(neighbours, distances, edge_mask, table, w_rbf, w_filter, layer, ready):
    inputs = (neighbours, distances, edge_mask, table, w_rbf, w_filter, ready)
    return pl.pallas_call(
        functools.partial(message_kernel, layer),
        out_shape=jax.ShapeDtypeStruct((neighbours.shape[1], table.shape[1]), BF),
        in_specs=[VM] * len(inputs),
        out_specs=VM,
        compiler_params=limit,
        name="messages",
    )(*inputs)


def gathered_field(places, rows, matrices, states):
    total = None
    for which, start, matrix, column in places:
        part = dot(
            matrices[matrix][:, column * rows : (column + 1) * rows], states[which][start : start + rows, :]
        )
        total = part if total is None else total + part
    return total


def partial_kernel(places, pairs, layer, message_ref, short_ref, mixing_ref, long_ref, *refs):
    matrices, states = refs[:pairs], refs[pairs:-3]
    total_ref, close_ref, joint_ref = refs[-3:]
    total_ref[...] = gathered_field(places, message_ref.shape[0], matrices, states)
    close_ref[...] = dot(message_ref[...], short_ref[layer])
    joint_ref[...] = dot(mixing_ref[layer], long_ref[layer]).astype(BF)


def partial_update(message, w_short, w_mixing, w_long, layer, matrices, arrays, places):
    shape = jax.ShapeDtypeStruct(message.shape, F32)
    return pl.pallas_call(
        functools.partial(partial_kernel, tuple(places), len(matrices), layer),
        out_shape=(shape, shape, jax.ShapeDtypeStruct(w_mixing.shape[1:], BF)),
        in_specs=[VM] * (4 + len(matrices) + len(arrays)),
        out_specs=(VM,) * 3,
        compiler_params=limit,
        name="partial",
    )(message, w_short, w_mixing, w_long, *matrices, *arrays)


def update_kernel(places, pairs, scale, own_ref, total_ref, close_ref, joint_ref, *refs):
    matrices, states, out_ref = refs[:pairs], refs[pairs:-1], refs[-1]
    total = total_ref[...] + gathered_field(places, own_ref.shape[0], matrices, states)
    half = 0.5 * (close_ref[...] + dot((total * scale).astype(BF), joint_ref[...]))
    out_ref[...] = (own_ref[...].astype(F32) + (half + half * jnp.tanh(half))).astype(BF)


def update(own, head, matrices, arrays, places, scale):
    return pl.pallas_call(
        functools.partial(update_kernel, tuple(places), len(matrices), scale),
        out_shape=jax.ShapeDtypeStruct(own.shape, BF),
        in_specs=[VM] * (4 + len(matrices) + len(arrays)),
        out_specs=VM,
        compiler_params=limit,
        name="update",
    )(own, *head, *matrices, *arrays)


def picked(spots, matrices, arrays):
    rows = sorted({spot[2] for spot in spots})
    used = sorted({spot[0] for spot in spots})
    spots = [(used.index(a), s, rows.index(m), c) for a, s, m, c in spots]
    return [matrices[m] for m in rows], [arrays[a] for a in used], spots


def swap(x, even, odd):
    count = lax.axis_size("atom")
    return lax.ppermute(x, "atom", [(i, i ^ (odd if i % 2 else even)) for i in range(count)])


def schedule(count, lean):
    bits = [1 << n for n in range(count.bit_length() - 1)][::-1]
    stages, have = [], [0]
    if len(bits) >= 4:
        far, near, side, last = bits[0], bits[1], bits[2], bits[-1]
        first = [far + near, far, near]
        early = first if lean else first + [side]
        sent = [0] + first if lean else first
        second = [side + q for q in sent]
        stages.append([(mask, mask, [0], [mask]) for mask in early + [last]])
        stages.append([(side, side, sent, second), (last, last, early, [last + q for q in early])])
        stages.append([(last, last, second, [last + q for q in second])])
        have = [0] + [q for stage in stages for item in stage for q in item[3]]
        bits = bits[3:-1]
    for bit in bits:
        stages.append([(bit, bit, list(have), [q ^ bit for q in have])])
        have = have + [q ^ bit for q in have]
    return stages


def exchange(arrays, places, stage, size):
    arrays, places = list(arrays), dict(places)
    sends = []
    for _, _, wanted, _ in stage:
        parts = [
            lax.slice_in_dim(arrays[places[q][0]], places[q][1], places[q][1] + size, axis=0)
            for q in wanted
        ]
        sends.append(parts[0] if len(parts) == 1 else jnp.concatenate(parts, axis=0))
    for (even, odd, _, labels), sent in zip(stage, sends):
        arrays.append(swap(sent, even, odd))
        for n, q in enumerate(labels):
            places[q] = (len(arrays) - 1, n * size)
    return arrays, places


def neighbour_table(own, close, even):
    count = lax.axis_size("atom")
    far = lax.ppermute(
        own, "atom", [(i, (i + (count - 1 if i % 2 == 0 else 1)) % count) for i in range(count)]
    )
    return jnp.concatenate([jnp.where(even, far, close), own, jnp.where(even, close, far)], axis=0)


def per_device(
    features,
    fractional,
    distances,
    neighbours,
    edge_mask,
    wave_index,
    w_rbf,
    w_filter,
    w_mixing,
    w_short,
    w_long,
):
    rows, _ = features.shape
    slots = neighbours.shape[0]
    bricks = lax.axis_size("atom")
    before = 1.0 / math.sqrt(rows * bricks)
    after = 4.0 / math.sqrt(wave_index.shape[1])
    even = lax.axis_index("atom") % 2 == 0

    packed, *prepared, near_distances, first_rbf, first_filter = prepare(
        wave_index, fractional, features, distances, w_rbf, w_filter
    )
    state = features
    matrices, where = [], {}

    def couple(arrays, places):
        ready = [q for q in places if q not in where]
        if len(places) < bricks:
            ready = ready[: len(ready) // 2 * 2]
        matrix = coupling_of(prepared, arrays, places, ready, rows)
        where.update({q: (len(matrices), n) for n, q in enumerate(ready)})
        matrices.append(matrix)

    for layer in range(w_rbf.shape[0]):
        block = state if layer else packed
        stages = schedule(bricks, False)
        size = block.shape[0]
        arrays, places = exchange([block], {0: (0, 0)}, stages[0], size)
        close = arrays[places[1][0]][:rows] if 1 in places else swap(state, 1, 1)
        table = neighbour_table(state, close, even)
        if layer:
            edge = (distances, w_rbf, w_filter, layer)
        else:
            edge = (near_distances, first_rbf, first_filter, 0)
        ready = filters_of(*edge, slots // 2)
        message = messages(neighbours, edge[0], edge_mask, table, *edge[1:], ready)
        for stage in stages[1:]:
            if layer == 0:
                couple(arrays, places)
            early = list(places)
            arrays, places = exchange(arrays, places, stage, size)
        early = [q for q in early if layer or q in where]
        spot = {q: places[q] + where[q] for q in early}
        used, held, spots = picked([spot[q] for q in early], matrices, arrays)
        head = partial_update(message, w_short, w_mixing, w_long, layer, used, held, spots)
        if layer == 0:
            couple(arrays, places)
        spot = {q: places[q] + where[q] for q in places if q not in early}
        used, held, spots = picked(list(spot.values()), matrices, arrays)
        state = update(state, head, used, held, spots, before * after)
    return state


def solution(mesh):
    along = P(None, ("rep", "atom"))
    in_specs = (P(("rep", "atom"), None), along, along, along, along) + (P(),) * 6
    return jax.shard_map(
        per_device, mesh=mesh, in_specs=in_specs, out_specs=P(("rep", "atom"), None), check_vma=False
    )
```
